512 devices in a mesh: scen: 8 (over x, core), bus: 64 (over y, z).
Axes of the slice: x: 4, y: 8, z: 8, core: 2. Of those that a mesh axis runs over, the one named last changes fastest.
Arguments:
- injections: bfloat16 [1024, 16384], P(('scen', 'bus')), may hold values from -6 to 6
- tile_values: bfloat16 [4096, 128, 128], P('bus', 'scen'), may hold values from -0.109375 to 0.109375
- tile_line: int32 [4096], P('bus'), may hold values from 0 to 191, as said below
- tile_bus: int32 [4096], P('bus'), may hold values from 0 to 1
- flow_pred: bfloat16 [1024, 24576], P('scen', 'bus'), may hold values from -6 to 6
- line_limit: int32 [24576], P('bus'), may hold values from 50 to 199
Outputs:
- grad_injections: bfloat16 [1024, 16384], P(('scen', 'bus'))
- flows: float32 [1024, 24576], P('scen', 'bus')
The draws below stay inside these ranges and needn't reach their ends.
Inputs may be any that keep to these rules, and one draw needn't show every extreme that they name: `tile_line`: tile t is held by bus index t // 64; line block b is owned by bus index b // 3. Of the 64 tiles of one bus index at most 2 have line blocks of one owner, and in every draw some owner gets exactly 2 tiles from every bus index. A pair of line block and bus block may occur in several tiles; their values add.
All inputs are finite; a program needn't handle non-finite values.
Results may differ from the reference program's by a relative error of at most 0.0039.
Values may be sent and summed in bfloat16 or wider, within the bound.
No kernel may reach another device: no remote copies, remote signals or barrier semaphores. Data moves between devices by JAX's collectives and lax.ppermute only.
A program may use at most 64 MiB of HBM per device.

```python
import jax
import jax.numpy as jnp
from jax import lax

TILE = 128
BB_DEV = 2
LB_DEV = 3
TILES_DEV = 64
CAP = 2
SCEN = 1024
NBUS = 16384
NLINE = 24576
NTILE = 4096
N_BUS = 64


def plan_source(source_key, source, hot_owner, base_offset):
    key_scores, key_shuffle = jax.random.split(source_key, 2)
    slot_total = N_BUS * CAP
    scores = jax.random.permutation(key_scores, slot_total).astype(jnp.int32)
    positions = jnp.arange(slot_total, dtype=jnp.int32)
    peer_index = positions // CAP
    copy_index = positions % CAP
    scores = jnp.where(peer_index == hot_owner, scores + 2 * slot_total, scores)
    forced = ((peer_index == 0) | (peer_index == N_BUS - 1)) & (copy_index == 0) & (peer_index != hot_owner)
    scores = jnp.where(forced, scores - 2 * slot_total, scores)
    ordering = jnp.argsort(scores)
    chosen = peer_index[ordering[:TILES_DEV - CAP]]
    destination = jnp.concatenate([jnp.full((CAP,), hot_owner, jnp.int32), chosen.astype(jnp.int32)])
    owner_hits = (destination[:, None] == jnp.arange(N_BUS, dtype=jnp.int32)[None, :]).astype(jnp.int32)
    rank_within = jnp.sum(jnp.cumsum(owner_hits, axis=0) * owner_hits, axis=1) - 1
    offset_here = (source + base_offset) % LB_DEV
    local_block = (rank_within + offset_here) % LB_DEV
    line_blocks = destination * LB_DEV + local_block
    shuffle = jax.random.permutation(key_shuffle, TILES_DEV)
    return line_blocks[shuffle]


def draw_tile_line(key, part):
    key_hot, key_base, key_rest = jax.random.split(jax.random.fold_in(key, 11), 3)
    hot_owner = jax.random.randint(key_hot, (), 0, N_BUS).astype(jnp.int32)
    base_offset = jax.random.randint(key_base, (), 0, LB_DEV).astype(jnp.int32)
    source_keys = jax.random.split(key_rest, N_BUS)
    sources = jnp.arange(N_BUS, dtype=jnp.int32)
    planned = jax.vmap(plan_source, in_axes=(0, 0, None, None))(source_keys, sources, hot_owner, base_offset)
    return planned.reshape(N_BUS * TILES_DEV).astype(jnp.int32)


def place_ends(array, rng, least, largest):
    longest = array.shape.index(max(array.shape))
    spots = []
    for shift in (0, 1):
        where = [jax.random.randint(jax.random.fold_in(rng, axis), (), 0, length) for axis, length in enumerate(array.shape)]
        where[longest] = (where[longest] + shift) % array.shape[longest]
        spots.append(tuple(where))
    return array.at[spots[0]].set(least).at[spots[1]].set(largest)


def block_levels(own_key, extent, pieces, smallest, largest):
    def one(dim, shards_of):
        draws = jax.random.uniform(jax.random.fold_in(jax.random.fold_in(own_key, 6), dim), (shards_of,), jnp.float32, smallest / len(pieces), largest / len(pieces))
        return jnp.repeat(jnp.exp(draws), extent[dim] // shards_of).reshape((-1,) + (1,) * (len(extent) - dim - 1))

    loudness = one(*pieces[0])
    for cut in pieces[1:]:
        loudness = loudness * one(*cut)
    return loudness


def bell_draw(rng, dims, scale, bound, shards=(), kind=jnp.bfloat16):
    entries = scale * jax.random.normal(rng, dims, jnp.float32)
    if shards:
        entries = entries * block_levels(rng, dims, shards, -0.22, 0.18)
    return jnp.clip(entries, -bound, bound).astype(kind)


def setup_inputs(seed: int = 0) -> dict:
    arg_keys = jax.random.split(jax.random.key(seed), 7)
    return {
        "injections": bell_draw(arg_keys[0], (SCEN, NBUS), 1.0, 6.0, ((0, 512),)),
        "tile_values": bell_draw(arg_keys[1], (NTILE, TILE, TILE), (TILE * TILES_DEV // LB_DEV) ** -0.5, 0.109375, ((0, 64), (1, 8))),
        "tile_line": draw_tile_line(jax.random.fold_in(arg_keys[6], 71), 0),
        "tile_bus": place_ends(jax.random.randint(arg_keys[3], (NTILE,), 0, BB_DEV), jax.random.fold_in(arg_keys[3], 1), 0, BB_DEV - 1).astype(jnp.int32),
        "flow_pred": bell_draw(arg_keys[4], (SCEN, NLINE), 1.0, 6.0, ((0, 8), (1, 64))),
        "line_limit": place_ends(jax.random.randint(arg_keys[5], (NLINE,), 50, 200), jax.random.fold_in(arg_keys[5], 1), 50, 199).astype(jnp.int32),
    }


def reference(injections, tile_values, tile_line, tile_bus, flow_pred, line_limit):
    scen_count = injections.shape[0]
    inj_blocks = injections.astype(jnp.float32).reshape(scen_count, N_BUS * BB_DEV, TILE)
    tile_float = tile_values.astype(jnp.float32).reshape(N_BUS, TILES_DEV, TILE, TILE)
    bus_global = (jnp.arange(N_BUS * TILES_DEV, dtype=jnp.int32) // TILES_DEV) * BB_DEV + tile_bus.astype(jnp.int32)
    lines_grouped = tile_line.astype(jnp.int32).reshape(N_BUS, TILES_DEV)
    buses_grouped = bus_global.reshape(N_BUS, TILES_DEV)

    def forward_step(flow_acc, inputs):
        tile_group, line_group, bus_group = inputs
        selected = jnp.take(inj_blocks, bus_group, axis=1)
        partial_flows = jnp.einsum("stb,tlb->stl", selected, tile_group, precision=lax.Precision.HIGHEST)
        return flow_acc.at[:, line_group, :].add(partial_flows), None

    flow_zero = jnp.zeros((scen_count, N_BUS * LB_DEV, TILE), jnp.float32)
    flow_acc, unused_a = lax.scan(forward_step, flow_zero, (tile_float, lines_grouped, buses_grouped))
    flows = flow_acc.reshape(scen_count, N_BUS * LB_DEV * TILE)
    line_cap = line_limit.astype(jnp.float32) * 0.01
    residual = flows - flow_pred.astype(jnp.float32)
    grad_flow = (residual + jax.nn.sigmoid(4.0 * (flows - line_cap)) - jax.nn.sigmoid(4.0 * (-flows - line_cap))).astype(jnp.bfloat16)
    grad_blocks = grad_flow.astype(jnp.float32).reshape(scen_count, N_BUS * LB_DEV, TILE)

    def backward_step(grad_acc, inputs):
        tile_group, line_group, bus_group = inputs
        selected = jnp.take(grad_blocks, line_group, axis=1)
        contrib = jnp.einsum("stl,tlb->stb", selected, tile_group, precision=lax.Precision.HIGHEST)
        return grad_acc.at[:, bus_group, :].add(contrib), None

    grad_zero = jnp.zeros((scen_count, N_BUS * BB_DEV, TILE), jnp.float32)
    grad_acc, unused_b = lax.scan(backward_step, grad_zero, (tile_float, lines_grouped, buses_grouped))
    grad_injections = grad_acc.reshape(scen_count, N_BUS * BB_DEV * TILE).astype(jnp.bfloat16)
    return grad_injections, flows
```

```python
import jax
import jax.numpy as jnp
from jax import lax
from jax.experimental import pallas as pl
from jax.experimental.pallas import tpu as pltpu
from jax.sharding import PartitionSpec as P

AXES = ("scen", "bus")
NX = 4
NC = 2
NY = 8
NZ = 8
TILE = 128
LB = 3
BB = 2
CAP = 2
F32 = jnp.float32
BF16 = jnp.bfloat16


def dev(x, c, y, z):
    return ((x % NX) * NC + c) * (NY * NZ) + (y % NY) * NZ + (z % NZ)


def pairs(fn):
    return [
        (dev(x, c, y, z), fn(x, c, y, z))
        for x in range(NX)
        for c in range(NC)
        for y in range(NY)
        for z in range(NZ)
    ]


def ring_groups():
    minor, major = [], []
    for x in range(NX):
        for c in range(NC):
            for q in range(8):
                along_z = [dev(x, c, q, w) for w in range(NZ)]
                along_y = [dev(x, c, w, q) for w in range(NY)]
                minor.append(along_z if c == 0 else along_y)
                major.append(along_y if c == 0 else along_z)
    return minor, major


MINOR, MAJOR = ring_groups()
X_UP = pairs(lambda x, c, y, z: dev(x + 1, c, y, z))
X_DOWN = pairs(lambda x, c, y, z: dev(x - 1, c, y, z))
CORE_SWAP = pairs(lambda x, c, y, z: dev(x, 1 - c, y, z))


def pack_kernel(line_ref, tiles_ref, out_ref, count_ref):
    out_ref[...] = jnp.zeros_like(out_ref)
    owners = count_ref.shape[0]
    for i in range(owners):
        count_ref[i] = 0

    def body(t, carry):
        owner = lax.div(line_ref[t], LB)
        rank = count_ref[owner]
        count_ref[owner] = rank + 1
        out_ref[owner * CAP + rank] = tiles_ref[t]
        return carry

    lax.fori_loop(0, tiles_ref.shape[0], body, 0, unroll=4)


def pack_tiles(tile_line, tile_values, owners):
    rows, lanes = tile_values.shape[1:]
    return pl.pallas_call(
        pack_kernel,
        out_shape=jax.ShapeDtypeStruct((owners * CAP, rows, lanes), tile_values.dtype),
        in_specs=[
            pl.BlockSpec(memory_space=pltpu.SMEM),
            pl.BlockSpec(memory_space=pltpu.VMEM),
        ],
        out_specs=pl.BlockSpec(memory_space=pltpu.VMEM),
        scratch_shapes=[pltpu.SMEM((owners,), jnp.int32)],
        name="pack_tiles",
    )(tile_line, tile_values)


def dot(a, b, dims):
    return lax.dot_general(a, b, (dims, ((), ())), preferred_element_type=F32)


NN = ((1,), (0,))
NT = ((1,), (1,))


def core_kernel(
    label_ref, x_ref, own_ref, other_ref, pred_ref, limit_ref, rowp_ref, colp_ref,
    flows_ref, c_ref, acc_ref, g_ref,
):
    sources = label_ref.shape[0] // CAP

    def tile(j):
        return jnp.concatenate(
            [own_ref[d, j] for d in range(NX)] + [other_ref[d, j] for d in range(NX)], axis=0
        )

    acc_ref[...] = jnp.zeros_like(acc_ref)

    def forward(s, carry):
        for r in range(CAP):
            j = s * CAP + r
            code = label_ref[j]
            line = code >> 1
            bus = code & 1
            start = pl.multiple_of((s * BB + bus) * TILE, TILE)
            part = dot(x_ref[:, pl.ds(start, TILE)], tile(j), NT)
            acc_ref[line] = acc_ref[line] + part
        return carry

    lax.fori_loop(0, sources, forward, 0, unroll=2)

    rowp = rowp_ref[...]
    colp = colp_ref[...]
    for b in range(LB):
        rest = acc_ref[b]
        flow = None
        for k in range(3):
            piece = rest.astype(BF16)
            rest = rest - piece.astype(F32)
            moved = dot(dot(rowp, piece, NN).astype(BF16), colp, NN)
            flow = moved if flow is None else flow + moved
        lanes = slice(b * TILE, (b + 1) * TILE)
        flows_ref[:, lanes] = flow
        cap = limit_ref[:, lanes].astype(F32) * 0.01
        grad = (
            (flow - pred_ref[:, lanes].astype(F32))
            + jax.nn.sigmoid(4.0 * (flow - cap))
            - jax.nn.sigmoid(4.0 * (-flow - cap))
        ).astype(BF16)
        grad = dot(rowp, grad, ((0,), (0,))).astype(BF16)
        g_ref[b] = dot(grad, colp, NT).astype(BF16)

    def backward(s, carry):
        low = jnp.zeros((g_ref.shape[1], TILE), F32)
        high = low
        for r in range(CAP):
            j = s * CAP + r
            code = label_ref[j]
            line = code >> 1
            bus = code & 1
            part = dot(g_ref[line], tile(j), NN)
            low = low + jnp.where(bus == 0, part, 0.0)
            high = high + jnp.where(bus == 1, part, 0.0)
        start = pl.multiple_of(s * BB * TILE, BB * TILE)
        c_ref[:, pl.ds(start, BB * TILE)] = jnp.concatenate([low, high], axis=1).astype(BF16)
        return carry

    lax.fori_loop(0, sources, backward, 0, unroll=2)


def core_call(labels, x, own, other, pred, limit, rowp, colp, nbus):
    rows, lines = pred.shape
    vmem = pl.BlockSpec(memory_space=pltpu.VMEM)
    return pl.pallas_call(
        core_kernel,
        out_shape=(
            jax.ShapeDtypeStruct((rows, lines), F32),
            jax.ShapeDtypeStruct((rows, nbus), BF16),
        ),
        in_specs=[pl.BlockSpec(memory_space=pltpu.SMEM)] + [vmem] * 7,
        out_specs=(vmem, vmem),
        scratch_shapes=[
            pltpu.VMEM((LB, rows, TILE), F32),
            pltpu.VMEM((LB, rows, TILE), BF16),
        ],
        compiler_params=pltpu.CompilerParams(vmem_limit_bytes=32 * 1024 * 1024),
        name="flows_and_grad",
    )(labels, x, own, other, pred, limit, rowp, colp)


def per_device(injections, tile_values, tile_line, tile_bus, flow_pred, line_limit):
    here = lax.axis_index("bus")
    scen = lax.axis_index("scen")
    x_here = scen // NC
    core = scen % NC
    buses = lax.axis_size("bus")
    rows_here, nbus = injections.shape
    count = tile_line.shape[0]

    packed = pack_tiles(tile_line, tile_values, buses)
    mine = lax.all_to_all(
        packed.reshape((buses, CAP) + packed.shape[1:]), "bus", split_axis=0, concat_axis=0, tiled=True
    ).reshape(packed.shape)

    owner = tile_line // LB
    inside = (tile_line % LB) * BB + tile_bus
    codes = jnp.pad(
        jnp.stack([owner, inside]), ((0, 0), (0, TILE - count)), constant_values=255
    ).astype(BF16)
    wide = jnp.concatenate([injections, codes], axis=1)
    near = lax.all_to_all(
        jnp.broadcast_to(wide[None], (8,) + wide.shape),
        AXES, split_axis=0, concat_axis=0, tiled=True, axis_index_groups=MINOR,
    ).reshape(8 * rows_here, wide.shape[1])
    x_all = lax.all_gather(near, AXES, axis=0, tiled=True, axis_index_groups=MAJOR)

    from_below = lax.ppermute(mine, AXES, X_UP)
    from_above = lax.ppermute(mine, AXES, X_DOWN)
    from_far = lax.ppermute(from_below, AXES, X_UP)
    own = jnp.stack([mine, from_above, from_far, from_below])
    other = lax.ppermute(own, AXES, CORE_SWAP)

    tags = x_all[:, nbus:].astype(jnp.int32).reshape(8, 8, rows_here, TILE)
    hit = tags[:, :, 0, :] == here
    inner = tags[:, :, 1, :]
    lane = lax.broadcasted_iota(jnp.int32, hit.shape, 2)
    first = jnp.min(jnp.where(hit, lane, TILE), axis=2, keepdims=True)
    code_first = jnp.sum(jnp.where(lane == first, inner, 0), axis=2)
    code_second = jnp.sum(jnp.where(hit, inner, 0), axis=2) - code_first
    labels = jnp.stack([code_first, code_second], axis=2)
    labels = jnp.where(core == 0, labels, jnp.swapaxes(labels, 0, 1)).reshape(buses * CAP)

    row = lax.broadcasted_iota(jnp.int32, (TILE, TILE), 0)
    col = lax.broadcasted_iota(jnp.int32, (TILE, TILE), 1)
    swapped = ((col // 2) % 8 * 8 + col // 16) * 2 + col % 2
    rowp = (row == jnp.where(core == 0, col, swapped)).astype(BF16)
    chunk = row // 16
    line_of = (((chunk % NX + x_here) % NX) * NC + jnp.where(chunk < NX, core, 1 - core)) * 16 + row % 16
    colp = (col == line_of).astype(BF16)

    flows, contrib = core_call(
        labels, x_all, own, other, flow_pred, line_limit.reshape(1, -1), rowp, colp, nbus
    )

    parts = lax.all_to_all(
        contrib.reshape(8, 8 * rows_here, nbus),
        AXES, split_axis=0, concat_axis=0, tiled=True, axis_index_groups=MAJOR,
    )
    half = jnp.sum(parts.astype(F32), axis=0)
    last = lax.all_to_all(
        half.reshape(8, rows_here, nbus),
        AXES, split_axis=0, concat_axis=0, tiled=True, axis_index_groups=MINOR,
    )
    grad_injections = jnp.sum(last, axis=0).astype(BF16)
    return (grad_injections, flows)


def solution(mesh):
    return jax.shard_map(
        per_device,
        mesh=mesh,
        in_specs=(
            P(("scen", "bus"), None),
            P("bus", "scen", None),
            P("bus"),
            P("bus"),
            P("scen", "bus"),
            P("bus"),
        ),
        out_specs=(P(("scen", "bus"), None), P("scen", "bus")),
        check_vma=False,
    )
```

```python
import jax
import jax.numpy as jnp
from jax import lax
from jax.experimental import pallas as pl
from jax.experimental.pallas import tpu as pltpu
from jax.sharding import PartitionSpec as P

AXES = ("scen", "bus")
NX = 4
NC = 2
NY = 8
NZ = 8
TILE = 128
LB = 3
BB = 2
CAP = 2
F32 = jnp.float32
BF16 = jnp.bfloat16


def dev(x, c, y, z):
    return ((x % NX) * NC + c) * (NY * NZ) + (y % NY) * NZ + (z % NZ)


def pairs(fn):
    return [
        (dev(x, c, y, z), fn(x, c, y, z))
        for x in range(NX)
        for c in range(NC)
        for y in range(NY)
        for z in range(NZ)
    ]


def ring_groups():
    minor, major = [], []
    for x in range(NX):
        for c in range(NC):
            for q in range(8):
                along_z = [dev(x, c, q, w) for w in range(NZ)]
                along_y = [dev(x, c, w, q) for w in range(NY)]
                minor.append(along_z if c == 0 else along_y)
                major.append(along_y if c == 0 else along_z)
    return minor, major


MINOR, MAJOR = ring_groups()
X_UP = pairs(lambda x, c, y, z: dev(x + 1, c, y, z))
X_DOWN = pairs(lambda x, c, y, z: dev(x - 1, c, y, z))
CORE_SWAP = pairs(lambda x, c, y, z: dev(x, 1 - c, y, z))


def pack_kernel(line_ref, tiles_ref, out_ref, count_ref):
    out_ref[...] = jnp.zeros_like(out_ref)
    owners = count_ref.shape[0]
    for i in range(owners):
        count_ref[i] = 0

    def body(t, carry):
        owner = lax.div(line_ref[t], LB)
        rank = count_ref[owner]
        count_ref[owner] = rank + 1
        out_ref[owner * CAP + rank] = tiles_ref[t]
        return carry

    lax.fori_loop(0, tiles_ref.shape[0], body, 0, unroll=4)


def pack_tiles(tile_line, tile_values, owners):
    rows, lanes = tile_values.shape[1:]
    return pl.pallas_call(
        pack_kernel,
        out_shape=jax.ShapeDtypeStruct((owners * CAP, rows, lanes), tile_values.dtype),
        in_specs=[
            pl.BlockSpec(memory_space=pltpu.SMEM),
            pl.BlockSpec(memory_space=pltpu.VMEM),
        ],
        out_specs=pl.BlockSpec(memory_space=pltpu.VMEM),
        scratch_shapes=[pltpu.SMEM((owners,), jnp.int32)],
        name="pack_tiles",
    )(tile_line, tile_values)


def dot(a, b, dims):
    return lax.dot_general(a, b, (dims, ((), ())), preferred_element_type=F32)


NN = ((1,), (0,))
NT = ((1,), (1,))


def core_kernel(
    label_ref, x_ref, own_ref, other_ref, pred_ref, limit_ref, rowp_ref, colp_ref,
    flows_ref, c_ref, acc_ref, g_ref,
):
    sources = label_ref.shape[0] // CAP

    def tile(j):
        return jnp.concatenate(
            [own_ref[d, j] for d in range(NX)] + [other_ref[d, j] for d in range(NX)], axis=0
        )

    acc_ref[...] = jnp.zeros_like(acc_ref)

    def forward(s, carry):
        for r in range(CAP):
            j = s * CAP + r
            code = label_ref[j]
            line = code >> 1
            bus = code & 1
            start = pl.multiple_of((s * BB + bus) * TILE, TILE)
            part = dot(x_ref[:, pl.ds(start, TILE)], tile(j), NT)
            acc_ref[line] = acc_ref[line] + part
        return carry

    lax.fori_loop(0, sources, forward, 0, unroll=2)

    rowp = rowp_ref[...]
    colp = colp_ref[...]
    for b in range(LB):
        rest = acc_ref[b]
        flow = None
        for k in range(3):
            piece = rest.astype(BF16)
            rest = rest - piece.astype(F32)
            moved = dot(dot(rowp, piece, NN).astype(BF16), colp, NN)
            flow = moved if flow is None else flow + moved
        lanes = slice(b * TILE, (b + 1) * TILE)
        flows_ref[:, lanes] = flow
        cap = limit_ref[:, lanes].astype(F32) * 0.01
        grad = (
            (flow - pred_ref[:, lanes].astype(F32))
            + jax.nn.sigmoid(4.0 * (flow - cap))
            - jax.nn.sigmoid(4.0 * (-flow - cap))
        ).astype(BF16)
        grad = dot(rowp, grad, ((0,), (0,))).astype(BF16)
        g_ref[b] = dot(grad, colp, NT).astype(BF16)

    def backward(s, carry):
        low = jnp.zeros((g_ref.shape[1], TILE), F32)
        high = low
        for r in range(CAP):
            j = s * CAP + r
            code = label_ref[j]
            line = code >> 1
            bus = code & 1
            part = dot(g_ref[line], tile(j), NN)
            low = low + jnp.where(bus == 0, part, 0.0)
            high = high + jnp.where(bus == 1, part, 0.0)
        start = pl.multiple_of(s * BB * TILE, BB * TILE)
        c_ref[:, pl.ds(start, BB * TILE)] = jnp.concatenate([low, high], axis=1).astype(BF16)
        return carry

    lax.fori_loop(0, sources, backward, 0, unroll=2)


def core_call(labels, x, own, other, pred, limit, rowp, colp, nbus):
    rows, lines = pred.shape
    vmem = pl.BlockSpec(memory_space=pltpu.VMEM)
    return pl.pallas_call(
        core_kernel,
        out_shape=(
            jax.ShapeDtypeStruct((rows, lines), F32),
            jax.ShapeDtypeStruct((rows, nbus), BF16),
        ),
        in_specs=[pl.BlockSpec(memory_space=pltpu.SMEM)] + [vmem] * 7,
        out_specs=(vmem, vmem),
        scratch_shapes=[
            pltpu.VMEM((LB, rows, TILE), F32),
            pltpu.VMEM((LB, rows, TILE), BF16),
        ],
        compiler_params=pltpu.CompilerParams(vmem_limit_bytes=32 * 1024 * 1024),
        name="flows_and_grad",
    )(labels, x, own, other, pred, limit, rowp, colp)


def per_device(injections, tile_values, tile_line, tile_bus, flow_pred, line_limit):
    here = lax.axis_index("bus")
    scen = lax.axis_index("scen")
    x_here = scen // NC
    core = scen % NC
    buses = lax.axis_size("bus")
    rows_here, nbus = injections.shape
    count = tile_line.shape[0]

    packed = pack_tiles(tile_line, tile_values, buses)
    mine = lax.all_to_all(
        packed.reshape((buses, CAP) + packed.shape[1:]), "bus", split_axis=0, concat_axis=0, tiled=True
    ).reshape(packed.shape)

    owner = tile_line // LB
    inside = (tile_line % LB) * BB + tile_bus
    codes = jnp.pad(
        jnp.stack([owner, inside]),
        ((0, nbus * rows_here // TILE - 2), (0, TILE - count)),
        constant_values=255,
    ).astype(BF16)
    blocks = nbus // TILE
    flat = injections.reshape(rows_here, blocks, TILE).swapaxes(0, 1).reshape(rows_here * blocks, TILE)
    wide = jnp.concatenate([flat, codes], axis=0)
    near = lax.all_gather(wide, AXES, axis=0, tiled=False, axis_index_groups=MINOR)
    near_x = near[:, : rows_here * blocks].reshape(8, blocks, rows_here, TILE).swapaxes(1, 2)
    near_code = near[:, rows_here * blocks : rows_here * blocks + 2].reshape(8 * 2, TILE)
    near = jnp.concatenate([near_x.reshape(8 * rows_here, nbus), near_code], axis=1)
    x_all = lax.all_gather(near, AXES, axis=0, tiled=True, axis_index_groups=MAJOR)

    from_below = lax.ppermute(mine, AXES, X_UP)
    from_above = lax.ppermute(mine, AXES, X_DOWN)
    from_far = lax.ppermute(from_below, AXES, X_UP)
    own = jnp.stack([mine, from_above, from_far, from_below])
    other = lax.ppermute(own, AXES, CORE_SWAP)

    tags = x_all[:, nbus:].astype(jnp.int32).reshape(8, 8, rows_here, TILE)
    hit = tags[:, :, 0, :] == here
    inner = tags[:, :, 1, :]
    lane = lax.broadcasted_iota(jnp.int32, hit.shape, 2)
    first = jnp.min(jnp.where(hit, lane, TILE), axis=2, keepdims=True)
    code_first = jnp.sum(jnp.where(lane == first, inner, 0), axis=2)
    code_second = jnp.sum(jnp.where(hit, inner, 0), axis=2) - code_first
    labels = jnp.stack([code_first, code_second], axis=2)
    labels = jnp.where(core == 0, labels, jnp.swapaxes(labels, 0, 1)).reshape(buses * CAP)

    row = lax.broadcasted_iota(jnp.int32, (TILE, TILE), 0)
    col = lax.broadcasted_iota(jnp.int32, (TILE, TILE), 1)
    swapped = ((col // 2) % 8 * 8 + col // 16) * 2 + col % 2
    rowp = (row == jnp.where(core == 0, col, swapped)).astype(BF16)
    chunk = row // 16
    line_of = (((chunk % NX + x_here) % NX) * NC + jnp.where(chunk < NX, core, 1 - core)) * 16 + row % 16
    colp = (col == line_of).astype(BF16)

    flows, contrib = core_call(
        labels, x_all, own, other, flow_pred, line_limit.reshape(1, -1), rowp, colp, nbus
    )

    parts = lax.all_to_all(
        contrib.reshape(8, 8 * rows_here, nbus),
        AXES, split_axis=0, concat_axis=0, tiled=True, axis_index_groups=MAJOR,
    )
    half = jnp.sum(parts.astype(F32), axis=0)
    last = lax.all_to_all(
        half.reshape(8, rows_here, nbus),
        AXES, split_axis=0, concat_axis=0, tiled=True, axis_index_groups=MINOR,
    )
    grad_injections = jnp.sum(last, axis=0).astype(BF16)
    return (grad_injections, flows)


def solution(mesh):
    return jax.shard_map(
        per_device,
        mesh=mesh,
        in_specs=(
            P(("scen", "bus"), None),
            P("bus", "scen", None),
            P("bus"),
            P("bus"),
            P("scen", "bus"),
            P("bus"),
        ),
        out_specs=(P(("scen", "bus"), None), P("scen", "bus")),
        check_vma=False,
    )
```

```python
import jax
import jax.numpy as jnp
from jax import lax
from jax.experimental import pallas as pl
from jax.experimental.pallas import tpu as pltpu
from jax.sharding import PartitionSpec as P

AXES = ("scen", "bus")
NX = 4
NC = 2
NY = 8
NZ = 8
TILE = 128
LB = 3
BB = 2
CAP = 2
F32 = jnp.float32
BF16 = jnp.bfloat16


def dev(x, c, y, z):
    return ((x % NX) * NC + c) * (NY * NZ) + (y % NY) * NZ + (z % NZ)


def pairs(fn):
    return [
        (dev(x, c, y, z), fn(x, c, y, z))
        for x in range(NX)
        for c in range(NC)
        for y in range(NY)
        for z in range(NZ)
    ]


def ring_groups():
    minor, major = [], []
    for x in range(NX):
        for c in range(NC):
            for q in range(8):
                along_z = [dev(x, c, q, w) for w in range(NZ)]
                along_y = [dev(x, c, w, q) for w in range(NY)]
                minor.append(along_z if c == 0 else along_y)
                major.append(along_y if c == 0 else along_z)
    return minor, major


MINOR, MAJOR = ring_groups()
X_UP = pairs(lambda x, c, y, z: dev(x + 1, c, y, z))
X_DOWN = pairs(lambda x, c, y, z: dev(x - 1, c, y, z))
CORE_SWAP = pairs(lambda x, c, y, z: dev(x, 1 - c, y, z))


def pack_kernel(core_ref, line_ref, tiles_ref, x_ref, code_ref, out_ref, count_ref):
    x_rows = x_ref.shape[0]
    head = x_rows + code_ref.shape[0]
    for m in range(out_ref.shape[0]):
        out_ref[m, :x_rows] = x_ref[...]
        out_ref[m, x_rows:head] = code_ref[...]
        out_ref[m, head:] = jnp.zeros((out_ref.shape[1] - head, TILE), out_ref.dtype)
    for i in range(count_ref.shape[0]):
        count_ref[i] = 0
    rows = tiles_ref.shape[1]
    first_core = core_ref[0] == 0

    def body(t, carry):
        owner = lax.div(line_ref[t], LB)
        rank = count_ref[owner]
        count_ref[owner] = rank + 1
        y = owner >> 3
        z = owner & 7
        minor = jnp.where(first_core, z, y)
        major = jnp.where(first_core, y, z)
        at = pl.multiple_of(head + (major * CAP + rank) * rows, rows)
        out_ref[minor, pl.ds(at, rows)] = tiles_ref[t]
        return carry

    lax.fori_loop(0, tiles_ref.shape[0], body, 0, unroll=4)


def pack(core, tile_line, tile_values, x, codes, owners):
    rows = tile_values.shape[1]
    total = x.shape[0] + codes.shape[0] + 8 * CAP * rows
    smem = pl.BlockSpec(memory_space=pltpu.SMEM)
    vmem = pl.BlockSpec(memory_space=pltpu.VMEM)
    return pl.pallas_call(
        pack_kernel,
        out_shape=jax.ShapeDtypeStruct((8, total, TILE), BF16),
        in_specs=[smem, smem, vmem, vmem, vmem],
        out_specs=vmem,
        scratch_shapes=[pltpu.SMEM((owners,), jnp.int32)],
        name="pack",
    )(core.reshape(1), tile_line, tile_values, x, codes)


def dot(a, b, dims):
    return lax.dot_general(a, b, (dims, ((), ())), preferred_element_type=F32)


NN = ((1,), (0,))
NT = ((1,), (1,))


def core_kernel(
    label_ref, x_ref, own_ref, other_ref, pred_ref, limit_ref, rowp_ref, colp_ref,
    flows_ref, c_ref, acc_ref, g_ref,
):
    sources = label_ref.shape[0] // CAP

    def tile(s, r):
        here = s * CAP + r
        there = ((s & 7) * 8 + (s >> 3)) * CAP + r
        return jnp.concatenate(
            [own_ref[d, here] for d in range(NX)] + [other_ref[d, there] for d in range(NX)], axis=0
        )

    acc_ref[...] = jnp.zeros_like(acc_ref)

    def forward(s, carry):
        for r in range(CAP):
            j = s * CAP + r
            code = label_ref[j]
            line = code & 3
            start = pl.multiple_of((code >> 2) * TILE, TILE)
            part = dot(x_ref[:, pl.ds(start, TILE)], tile(s, r), NT)
            acc_ref[line] = acc_ref[line] + part
        return carry

    lax.fori_loop(0, sources, forward, 0, unroll=2)

    rowp = rowp_ref[...]
    colp = colp_ref[...]
    for b in range(LB):
        rest = acc_ref[b]
        flow = None
        for k in range(3):
            piece = rest.astype(BF16)
            rest = rest - piece.astype(F32)
            moved = dot(dot(rowp, piece, NN).astype(BF16), colp, NN)
            flow = moved if flow is None else flow + moved
        lanes = slice(b * TILE, (b + 1) * TILE)
        flows_ref[:, lanes] = flow
        cap = limit_ref[:, lanes].astype(F32) * 0.01
        grad = (
            (flow - pred_ref[:, lanes].astype(F32))
            + jax.nn.sigmoid(4.0 * (flow - cap))
            - jax.nn.sigmoid(4.0 * (-flow - cap))
        ).astype(BF16)
        grad = dot(rowp, grad, ((0,), (0,))).astype(BF16)
        g_ref[b] = dot(grad, colp, NT).astype(BF16)

    def backward(s, carry):
        low = jnp.zeros((g_ref.shape[1], TILE), F32)
        high = low
        for r in range(CAP):
            j = s * CAP + r
            code = label_ref[j]
            line = code & 3
            bus = (code >> 2) & 1
            part = dot(g_ref[line], tile(s, r), NN)
            low = low + jnp.where(bus == 0, part, 0.0)
            high = high + jnp.where(bus == 1, part, 0.0)
        start = pl.multiple_of((label_ref[s * CAP] >> 3) * (BB * TILE), BB * TILE)
        c_ref[:, pl.ds(start, BB * TILE)] = jnp.concatenate([low, high], axis=1).astype(BF16)
        return carry

    lax.fori_loop(0, sources, backward, 0, unroll=2)


def core_call(labels, x, own, other, pred, limit, rowp, colp, nbus):
    rows, lines = pred.shape
    vmem = pl.BlockSpec(memory_space=pltpu.VMEM)
    return pl.pallas_call(
        core_kernel,
        out_shape=(
            jax.ShapeDtypeStruct((rows, lines), F32),
            jax.ShapeDtypeStruct((rows, nbus), BF16),
        ),
        in_specs=[pl.BlockSpec(memory_space=pltpu.SMEM)] + [vmem] * 7,
        out_specs=(vmem, vmem),
        scratch_shapes=[
            pltpu.VMEM((LB, rows, TILE), F32),
            pltpu.VMEM((LB, rows, TILE), BF16),
        ],
        compiler_params=pltpu.CompilerParams(vmem_limit_bytes=32 * 1024 * 1024),
        name="flows_and_grad",
    )(labels, x, own, other, pred, limit, rowp, colp)


def per_device(injections, tile_values, tile_line, tile_bus, flow_pred, line_limit):
    here = lax.axis_index("bus")
    scen = lax.axis_index("scen")
    x_here = scen // NC
    core = scen % NC
    buses = lax.axis_size("bus")
    rows_here, nbus = injections.shape
    count = tile_line.shape[0]

    owner = tile_line // LB
    inside = (tile_line % LB) * BB + tile_bus
    codes = jnp.pad(
        jnp.stack([owner, inside]), ((0, 14), (0, TILE - count)), constant_values=255
    ).astype(BF16)
    blocks = nbus // TILE
    x_rows = rows_here * blocks
    flat = injections.reshape(rows_here, blocks, TILE).swapaxes(0, 1).reshape(x_rows, TILE)
    packed = pack(core, tile_line, tile_values, flat, codes, buses)
    hop = lax.all_to_all(
        packed, AXES, split_axis=0, concat_axis=0, tiled=True, axis_index_groups=MINOR
    )
    near_x = hop[:, :x_rows].reshape(8, blocks, rows_here, TILE).swapaxes(1, 2)
    near_code = hop[:, x_rows : x_rows + rows_here].reshape(8 * rows_here, TILE)
    near = jnp.concatenate([near_x.reshape(8 * rows_here, nbus), near_code], axis=1)
    x_all = lax.all_gather(near, AXES, axis=0, tiled=True, axis_index_groups=MAJOR)

    slots = hop[:, x_rows + codes.shape[0] :].reshape((8, 8, CAP) + tile_values.shape[1:])
    mine = lax.all_to_all(
        slots.swapaxes(0, 1), AXES, split_axis=0, concat_axis=0, tiled=True, axis_index_groups=MAJOR
    ).reshape((buses * CAP,) + tile_values.shape[1:])
    from_below = lax.ppermute(mine, AXES, X_UP)
    from_above = lax.ppermute(mine, AXES, X_DOWN)
    from_far = lax.ppermute(from_below, AXES, X_UP)
    own = jnp.stack([mine, from_above, from_far, from_below])
    other = lax.ppermute(own, AXES, CORE_SWAP)

    tags = x_all[:, nbus:].astype(jnp.int32).reshape(buses, rows_here, TILE)
    hit = tags[:, 0, :] == here
    inner = tags[:, 1, :]
    lane = lax.broadcasted_iota(jnp.int32, hit.shape, 1)
    first = jnp.min(jnp.where(hit, lane, TILE), axis=1, keepdims=True)
    code_first = jnp.sum(jnp.where(lane == first, inner, 0), axis=1, keepdims=True)
    code_second = jnp.sum(jnp.where(hit, inner, 0), axis=1, keepdims=True) - code_first
    inner = jnp.concatenate([code_first, code_second], axis=1)
    order = lax.broadcasted_iota(jnp.int32, inner.shape, 0)
    source = jnp.where(core == 0, order, (order & 7) * 8 + (order >> 3))
    labels = (((source * BB + (inner & 1)) << 2) + (inner >> 1)).reshape(buses * CAP)

    row = lax.broadcasted_iota(jnp.int32, (TILE, TILE), 0)
    col = lax.broadcasted_iota(jnp.int32, (TILE, TILE), 1)
    swapped = ((col // 2) % 8 * 8 + col // 16) * 2 + col % 2
    rowp = (row == jnp.where(core == 0, col, swapped)).astype(BF16)
    chunk = row // 16
    line_of = (((chunk % NX + x_here) % NX) * NC + jnp.where(chunk < NX, core, 1 - core)) * 16 + row % 16
    colp = (col == line_of).astype(BF16)

    flows, contrib = core_call(
        labels, x_all, own, other, flow_pred, line_limit.reshape(1, -1), rowp, colp, nbus
    )

    parts = lax.all_to_all(
        contrib.reshape(8, 8 * rows_here, nbus),
        AXES, split_axis=0, concat_axis=0, tiled=True, axis_index_groups=MAJOR,
    )
    half = jnp.sum(parts.astype(F32), axis=0).astype(BF16)
    last = lax.all_to_all(
        half.reshape(8, rows_here, nbus),
        AXES, split_axis=0, concat_axis=0, tiled=True, axis_index_groups=MINOR,
    )
    grad_injections = jnp.sum(last.astype(F32), axis=0).astype(BF16)
    return (grad_injections, flows)


def solution(mesh):
    return jax.shard_map(
        per_device,
        mesh=mesh,
        in_specs=(
            P(("scen", "bus"), None),
            P("bus", "scen", None),
            P("bus"),
            P("bus"),
            P("scen", "bus"),
            P("bus"),
        ),
        out_specs=(P(("scen", "bus"), None), P("scen", "bus")),
        check_vma=False,
    )
```

```python
import jax
import jax.numpy as jnp
from jax import lax
from jax.experimental import pallas as pl
from jax.experimental.pallas import tpu as pltpu
from jax.sharding import PartitionSpec as P

AXES = ("scen", "bus")
NX = 4
NC = 2
NY = 8
NZ = 8
TILE = 128
LB = 3
BB = 2
CAP = 2
F32 = jnp.float32
BF16 = jnp.bfloat16


def dev(x, c, y, z):
    return ((x % NX) * NC + c) * (NY * NZ) + (y % NY) * NZ + (z % NZ)


def pairs(fn):
    return [
        (dev(x, c, y, z), fn(x, c, y, z))
        for x in range(NX)
        for c in range(NC)
        for y in range(NY)
        for z in range(NZ)
    ]


def ring_groups():
    minor, major = [], []
    for x in range(NX):
        for c in range(NC):
            for q in range(8):
                along_z = [dev(x, c, q, w) for w in range(NZ)]
                along_y = [dev(x, c, w, q) for w in range(NY)]
                minor.append(along_z if c == 0 else along_y)
                major.append(along_y if c == 0 else along_z)
    return minor, major


MINOR, MAJOR = ring_groups()
X_UP = pairs(lambda x, c, y, z: dev(x + 1, c, y, z))
X_DOWN = pairs(lambda x, c, y, z: dev(x - 1, c, y, z))
CORE_SWAP = pairs(lambda x, c, y, z: dev(x, 1 - c, y, z))


def pack_kernel(core_ref, line_ref, tiles_ref, x_ref, code_ref, out_ref, count_ref):
    x_rows = x_ref.shape[0]
    head = x_rows + code_ref.shape[0]
    for m in range(out_ref.shape[0]):
        out_ref[m, :x_rows] = x_ref[...]
        out_ref[m, x_rows:head] = code_ref[...]
        out_ref[m, head:] = jnp.zeros((out_ref.shape[1] - head, TILE), out_ref.dtype)
    for i in range(count_ref.shape[0]):
        count_ref[i] = 0
    rows = tiles_ref.shape[1]
    first_core = core_ref[0] == 0

    def body(t, carry):
        owner = lax.div(line_ref[t], LB)
        rank = count_ref[owner]
        count_ref[owner] = rank + 1
        y = owner >> 3
        z = owner & 7
        minor = jnp.where(first_core, z, y)
        major = jnp.where(first_core, y, z)
        at = pl.multiple_of(head + (major * CAP + rank) * rows, rows)
        out_ref[minor, pl.ds(at, rows)] = tiles_ref[t]
        return carry

    lax.fori_loop(0, tiles_ref.shape[0], body, 0, unroll=4)


def pack(core, tile_line, tile_values, x, codes, owners):
    rows = tile_values.shape[1]
    total = x.shape[0] + codes.shape[0] + 8 * CAP * rows
    smem = pl.BlockSpec(memory_space=pltpu.SMEM)
    vmem = pl.BlockSpec(memory_space=pltpu.VMEM)
    return pl.pallas_call(
        pack_kernel,
        out_shape=jax.ShapeDtypeStruct((8, total, TILE), BF16),
        in_specs=[smem, smem, vmem, vmem, vmem],
        out_specs=vmem,
        scratch_shapes=[pltpu.SMEM((owners,), jnp.int32)],
        name="pack",
    )(core.reshape(1), tile_line, tile_values, x, codes)


def dot(a, b, dims):
    return lax.dot_general(a, b, (dims, ((), ())), preferred_element_type=F32)


NN = ((1,), (0,))
NT = ((1,), (1,))


def core_kernel(
    label_ref, x_ref, own_ref, other_ref, pred_ref, limit_ref, rowp_ref, colp_ref,
    flows_ref, c_ref, acc_ref, g_ref,
):
    sources = label_ref.shape[0] // CAP

    def tile(s, r):
        here = s * CAP + r
        there = ((s & 7) * 8 + (s >> 3)) * CAP + r
        return jnp.concatenate(
            [own_ref[d, here] for d in range(NX)] + [other_ref[d, there] for d in range(NX)], axis=0
        )

    acc_ref[...] = jnp.zeros_like(acc_ref)

    def forward(s, carry):
        for r in range(CAP):
            j = s * CAP + r
            code = label_ref[j]
            line = code & 3
            start = pl.multiple_of((code >> 2) * TILE, TILE)
            part = dot(x_ref[:, pl.ds(start, TILE)], tile(s, r), NT)
            acc_ref[line] = acc_ref[line] + part
        return carry

    lax.fori_loop(0, sources, forward, 0, unroll=8)

    rowp = rowp_ref[...]
    colp = colp_ref[...]
    for b in range(LB):
        rest = acc_ref[b]
        flow = None
        for k in range(3):
            piece = rest.astype(BF16)
            rest = rest - piece.astype(F32)
            moved = dot(dot(rowp, piece, NN).astype(BF16), colp, NN)
            flow = moved if flow is None else flow + moved
        lanes = slice(b * TILE, (b + 1) * TILE)
        flows_ref[:, lanes] = flow
        cap = limit_ref[:, lanes].astype(F32) * 0.01
        grad = (
            (flow - pred_ref[:, lanes].astype(F32))
            + jax.nn.sigmoid(4.0 * (flow - cap))
            - jax.nn.sigmoid(4.0 * (-flow - cap))
        ).astype(BF16)
        grad = dot(rowp, grad, ((0,), (0,))).astype(BF16)
        g_ref[b] = dot(grad, colp, NT).astype(BF16)

    def backward(s, carry):
        low = jnp.zeros((g_ref.shape[1], TILE), F32)
        high = low
        for r in range(CAP):
            j = s * CAP + r
            code = label_ref[j]
            line = code & 3
            bus = (code >> 2) & 1
            part = dot(g_ref[line], tile(s, r), NN)
            low = low + jnp.where(bus == 0, part, 0.0)
            high = high + jnp.where(bus == 1, part, 0.0)
        start = pl.multiple_of((label_ref[s * CAP] >> 3) * (BB * TILE), BB * TILE)
        c_ref[:, pl.ds(start, BB * TILE)] = jnp.concatenate([low, high], axis=1).astype(BF16)
        return carry

    lax.fori_loop(0, sources, backward, 0, unroll=8)


def core_call(labels, x, own, other, pred, limit, rowp, colp, nbus):
    rows, lines = pred.shape
    vmem = pl.BlockSpec(memory_space=pltpu.VMEM)
    return pl.pallas_call(
        core_kernel,
        out_shape=(
            jax.ShapeDtypeStruct((rows, lines), F32),
            jax.ShapeDtypeStruct((rows, nbus), BF16),
        ),
        in_specs=[pl.BlockSpec(memory_space=pltpu.SMEM)] + [vmem] * 7,
        out_specs=(vmem, vmem),
        scratch_shapes=[
            pltpu.VMEM((LB, rows, TILE), F32),
            pltpu.VMEM((LB, rows, TILE), BF16),
        ],
        compiler_params=pltpu.CompilerParams(vmem_limit_bytes=32 * 1024 * 1024),
        name="flows_and_grad",
    )(labels, x, own, other, pred, limit, rowp, colp)


def add_up(parts):
    total = parts[0].astype(F32)
    for k in range(1, parts.shape[0]):
        total = total + parts[k].astype(F32)
    return total.astype(BF16)


def per_device(injections, tile_values, tile_line, tile_bus, flow_pred, line_limit):
    here = lax.axis_index("bus")
    scen = lax.axis_index("scen")
    x_here = scen // NC
    core = scen % NC
    buses = lax.axis_size("bus")
    rows_here, nbus = injections.shape
    count = tile_line.shape[0]

    owner = tile_line // LB
    inside = (tile_line % LB) * BB + tile_bus
    codes = jnp.pad(
        jnp.stack([owner, inside]), ((0, 14), (0, TILE - count)), constant_values=255
    ).astype(BF16)
    blocks = nbus // TILE
    x_rows = rows_here * blocks
    flat = injections.reshape(rows_here, blocks, TILE).swapaxes(0, 1).reshape(x_rows, TILE)
    packed = pack(core, tile_line, tile_values, flat, codes, buses)
    hop = lax.all_to_all(
        packed, AXES, split_axis=0, concat_axis=0, tiled=True, axis_index_groups=MINOR
    )
    near_x = hop[:, :x_rows].reshape(8, blocks, rows_here, TILE).swapaxes(1, 2)
    near_code = hop[:, x_rows : x_rows + rows_here].reshape(8 * rows_here, TILE)
    near = jnp.concatenate([near_x.reshape(8 * rows_here, nbus), near_code], axis=1)
    x_all = lax.all_gather(near, AXES, axis=0, tiled=True, axis_index_groups=MAJOR)

    slots = hop[:, x_rows + codes.shape[0] :].reshape((8, 8, CAP) + tile_values.shape[1:])
    mine = lax.all_to_all(
        slots.swapaxes(0, 1), AXES, split_axis=0, concat_axis=0, tiled=True, axis_index_groups=MAJOR
    ).reshape((buses * CAP,) + tile_values.shape[1:])
    from_below = lax.ppermute(mine, AXES, X_UP)
    from_above = lax.ppermute(mine, AXES, X_DOWN)
    from_far = lax.ppermute(from_below, AXES, X_UP)
    own = jnp.stack([mine, from_above, from_far, from_below])
    other = lax.ppermute(own, AXES, CORE_SWAP)

    tags = x_all[:, nbus:].astype(jnp.int32).reshape(buses, rows_here, TILE)
    hit = tags[:, 0, :] == here
    inner = tags[:, 1, :]
    lane = lax.broadcasted_iota(jnp.int32, hit.shape, 1)
    first = jnp.min(jnp.where(hit, lane, TILE), axis=1, keepdims=True)
    code_first = jnp.sum(jnp.where(lane == first, inner, 0), axis=1, keepdims=True)
    code_second = jnp.sum(jnp.where(hit, inner, 0), axis=1, keepdims=True) - code_first
    inner = jnp.concatenate([code_first, code_second], axis=1)
    order = lax.broadcasted_iota(jnp.int32, inner.shape, 0)
    source = jnp.where(core == 0, order, (order & 7) * 8 + (order >> 3))
    labels = (((source * BB + (inner & 1)) << 2) + (inner >> 1)).reshape(buses * CAP)

    row = lax.broadcasted_iota(jnp.int32, (TILE, TILE), 0)
    col = lax.broadcasted_iota(jnp.int32, (TILE, TILE), 1)
    swapped = ((col // 2) % 8 * 8 + col // 16) * 2 + col % 2
    rowp = (row == jnp.where(core == 0, col, swapped)).astype(BF16)
    chunk = row // 16
    line_of = (((chunk % NX + x_here) % NX) * NC + jnp.where(chunk < NX, core, 1 - core)) * 16 + row % 16
    colp = (col == line_of).astype(BF16)

    flows, contrib = core_call(
        labels, x_all, own, other, flow_pred, line_limit.reshape(1, -1), rowp, colp, nbus
    )

    parts = lax.all_to_all(
        contrib.reshape(8, 8 * rows_here, nbus),
        AXES, split_axis=0, concat_axis=0, tiled=True, axis_index_groups=MAJOR,
    )
    half = add_up(parts)
    last = lax.all_to_all(
        half.reshape(8, rows_here, nbus),
        AXES, split_axis=0, concat_axis=0, tiled=True, axis_index_groups=MINOR,
    )
    grad_injections = add_up(last)
    return (grad_injections, flows)


def solution(mesh):
    return jax.shard_map(
        per_device,
        mesh=mesh,
        in_specs=(
            P(("scen", "bus"), None),
            P("bus", "scen", None),
            P("bus"),
            P("bus"),
            P("scen", "bus"),
            P("bus"),
        ),
        out_specs=(P(("scen", "bus"), None), P("scen", "bus")),
        check_vma=False,
    )
```

```python
import jax
import jax.numpy as jnp
from jax import lax
from jax.experimental import pallas as pl
from jax.experimental.pallas import tpu as pltpu
from jax.sharding import PartitionSpec as P

AXES = ("scen", "bus")
NX = 4
NC = 2
NY = 8
NZ = 8
TILE = 128
LB = 3
BB = 2
CAP = 2
F32 = jnp.float32
BF16 = jnp.bfloat16


def dev(x, c, y, z):
    return ((x % NX) * NC + c) * (NY * NZ) + (y % NY) * NZ + (z % NZ)


def pairs(fn):
    return [
        (dev(x, c, y, z), fn(x, c, y, z))
        for x in range(NX)
        for c in range(NC)
        for y in range(NY)
        for z in range(NZ)
    ]


def ring_groups():
    minor, major = [], []
    for x in range(NX):
        for c in range(NC):
            for q in range(8):
                along_z = [dev(x, c, q, w) for w in range(NZ)]
                along_y = [dev(x, c, w, q) for w in range(NY)]
                minor.append(along_z if c == 0 else along_y)
                major.append(along_y if c == 0 else along_z)
    return minor, major


MINOR, MAJOR = ring_groups()
X_UP = pairs(lambda x, c, y, z: dev(x + 1, c, y, z))
X_DOWN = pairs(lambda x, c, y, z: dev(x - 1, c, y, z))
CORE_SWAP = pairs(lambda x, c, y, z: dev(x, 1 - c, y, z))


def pack_kernel(core_ref, line_ref, tiles_ref, x_ref, code_ref, out_ref, count_ref):
    x_rows = x_ref.shape[0]
    head = x_rows + code_ref.shape[0]
    for m in range(out_ref.shape[0]):
        out_ref[m, :x_rows] = x_ref[...]
        out_ref[m, x_rows:head] = code_ref[...]
        out_ref[m, head:] = jnp.zeros((out_ref.shape[1] - head, TILE), out_ref.dtype)
    for i in range(count_ref.shape[0]):
        count_ref[i] = 0
    rows = tiles_ref.shape[1]
    first_core = core_ref[0] == 0

    def body(t, carry):
        owner = lax.div(line_ref[t], LB)
        rank = count_ref[owner]
        count_ref[owner] = rank + 1
        y = owner >> 3
        z = owner & 7
        minor = jnp.where(first_core, z, y)
        major = jnp.where(first_core, y, z)
        at = pl.multiple_of(head + (major * CAP + rank) * rows, rows)
        out_ref[minor, pl.ds(at, rows)] = tiles_ref[t]
        return carry

    lax.fori_loop(0, tiles_ref.shape[0], body, 0, unroll=4)


def pack(core, tile_line, tile_values, x, codes, owners):
    rows = tile_values.shape[1]
    total = x.shape[0] + codes.shape[0] + 8 * CAP * rows
    smem = pl.BlockSpec(memory_space=pltpu.SMEM)
    vmem = pl.BlockSpec(memory_space=pltpu.VMEM)
    return pl.pallas_call(
        pack_kernel,
        out_shape=jax.ShapeDtypeStruct((8, total, TILE), BF16),
        in_specs=[smem, smem, vmem, vmem, vmem],
        out_specs=vmem,
        scratch_shapes=[pltpu.SMEM((owners,), jnp.int32)],
        name="pack",
    )(core.reshape(1), tile_line, tile_values, x, codes)


def dot(a, b, dims):
    return lax.dot_general(a, b, (dims, ((), ())), preferred_element_type=F32)


NN = ((1,), (0,))
NT = ((1,), (1,))


def core_kernel(
    label_ref, x_ref, own_ref, other_ref, pred_ref, limit_ref, rowp_ref, colp_ref,
    flows_ref, c_ref, acc_ref, g_ref,
):
    sources = label_ref.shape[0] // CAP

    def tile(s, r):
        here = s * CAP + r
        there = ((s & 7) * 8 + (s >> 3)) * CAP + r
        return jnp.concatenate(
            [own_ref[d, here] for d in range(NX)] + [other_ref[d, there] for d in range(NX)], axis=0
        )

    acc_ref[...] = jnp.zeros_like(acc_ref)

    def forward(s, carry):
        for r in range(CAP):
            j = s * CAP + r
            code = label_ref[j]
            line = code & 3
            start = pl.multiple_of((code >> 2) * TILE, TILE)
            part = dot(x_ref[:, pl.ds(start, TILE)], tile(s, r), NT)
            acc_ref[line] = acc_ref[line] + part
        return carry

    lax.fori_loop(0, sources, forward, 0, unroll=8)

    rowp = rowp_ref[...]
    colp = colp_ref[...]
    for b in range(LB):
        rest = acc_ref[b]
        flow = None
        for k in range(3):
            piece = rest.astype(BF16)
            rest = rest - piece.astype(F32)
            moved = dot(dot(rowp, piece, NN).astype(BF16), colp, NN)
            flow = moved if flow is None else flow + moved
        lanes = slice(b * TILE, (b + 1) * TILE)
        flows_ref[:, lanes] = flow
        cap = limit_ref[:, lanes].astype(F32) * 0.01
        grad = (
            (flow - pred_ref[:, lanes].astype(F32))
            + jax.nn.sigmoid(4.0 * (flow - cap))
            - jax.nn.sigmoid(4.0 * (-flow - cap))
        ).astype(BF16)
        grad = dot(rowp, grad, ((0,), (0,))).astype(BF16)
        g_ref[b] = dot(grad, colp, NT).astype(BF16)

    def backward(s, carry):
        low = jnp.zeros((g_ref.shape[1], TILE), F32)
        high = low
        for r in range(CAP):
            j = s * CAP + r
            code = label_ref[j]
            line = code & 3
            bus = (code >> 2) & 1
            part = dot(g_ref[line], tile(s, r), NN)
            low = low + jnp.where(bus == 0, part, 0.0)
            high = high + jnp.where(bus == 1, part, 0.0)
        start = pl.multiple_of((label_ref[s * CAP] >> 3) * (BB * TILE), BB * TILE)
        c_ref[:, pl.ds(start, BB * TILE)] = jnp.concatenate([low, high], axis=1).astype(BF16)
        return carry

    lax.fori_loop(0, sources, backward, 0, unroll=8)


def core_call(labels, x, own, other, pred, limit, rowp, colp, nbus):
    rows, lines = pred.shape
    vmem = pl.BlockSpec(memory_space=pltpu.VMEM)
    return pl.pallas_call(
        core_kernel,
        out_shape=(
            jax.ShapeDtypeStruct((rows, lines), F32),
            jax.ShapeDtypeStruct((rows, nbus), BF16),
        ),
        in_specs=[pl.BlockSpec(memory_space=pltpu.SMEM)] + [vmem] * 7,
        out_specs=(vmem, vmem),
        scratch_shapes=[
            pltpu.VMEM((LB, rows, TILE), F32),
            pltpu.VMEM((LB, rows, TILE), BF16),
        ],
        compiler_params=pltpu.CompilerParams(vmem_limit_bytes=32 * 1024 * 1024),
        name="flows_and_grad",
    )(labels, x, own, other, pred, limit, rowp, colp)


def add_up(parts):
    total = parts[0].astype(F32)
    for k in range(1, parts.shape[0]):
        total = total + parts[k].astype(F32)
    return total.astype(BF16)


def per_device(injections, tile_values, tile_line, tile_bus, flow_pred, line_limit):
    here = lax.axis_index("bus")
    scen = lax.axis_index("scen")
    x_here = scen // NC
    core = scen % NC
    buses = lax.axis_size("bus")
    rows_here, nbus = injections.shape
    count = tile_line.shape[0]

    owner = tile_line // LB
    inside = (tile_line % LB) * BB + tile_bus
    codes = jnp.pad(
        jnp.stack([owner, inside]), ((0, 14), (0, TILE - count)), constant_values=255
    ).astype(BF16)
    blocks = nbus // TILE
    x_rows = rows_here * blocks
    flat = injections.reshape(rows_here, blocks, TILE).swapaxes(0, 1).reshape(x_rows, TILE)
    packed = pack(core, tile_line, tile_values, flat, codes, buses)
    hop = lax.all_to_all(
        packed, AXES, split_axis=0, concat_axis=0, tiled=True, axis_index_groups=MINOR
    )
    near_x = hop[:, :x_rows].reshape(8, blocks, rows_here, TILE).swapaxes(1, 2)
    near_code = hop[:, x_rows : x_rows + rows_here].reshape(8 * rows_here, TILE)
    near = jnp.concatenate([near_x.reshape(8 * rows_here, nbus), near_code], axis=1)
    x_all = lax.all_gather(near, AXES, axis=0, tiled=True, axis_index_groups=MAJOR)

    slots = hop[:, x_rows + codes.shape[0] :].reshape((8, 8, CAP) + tile_values.shape[1:])
    mine = lax.all_to_all(
        slots.swapaxes(0, 1), AXES, split_axis=0, concat_axis=0, tiled=True, axis_index_groups=MAJOR
    ).reshape((buses * CAP,) + tile_values.shape[1:])
    from_below = lax.ppermute(mine, AXES, X_UP)
    from_above = lax.ppermute(mine, AXES, X_DOWN)
    from_far = lax.ppermute(from_below, AXES, X_UP)
    own = jnp.stack([mine, from_above, from_far, from_below])
    other = lax.ppermute(own, AXES, CORE_SWAP)

    tags = x_all[:, nbus:].astype(jnp.int32).reshape(buses, rows_here, TILE)
    hit = tags[:, 0, :] == here
    inner = tags[:, 1, :]
    lane = lax.broadcasted_iota(jnp.int32, hit.shape, 1)
    first = jnp.min(jnp.where(hit, lane, TILE), axis=1, keepdims=True)
    code_first = jnp.sum(jnp.where(lane == first, inner, 0), axis=1, keepdims=True)
    code_second = jnp.sum(jnp.where(hit, inner, 0), axis=1, keepdims=True) - code_first
    inner = jnp.concatenate([code_first, code_second], axis=1)
    order = lax.broadcasted_iota(jnp.int32, inner.shape, 0)
    source = jnp.where(core == 0, order, (order & 7) * 8 + (order >> 3))
    labels = (((source * BB + (inner & 1)) << 2) + (inner >> 1)).reshape(buses * CAP)

    row = lax.broadcasted_iota(jnp.int32, (TILE, TILE), 0)
    col = lax.broadcasted_iota(jnp.int32, (TILE, TILE), 1)
    swapped = ((col // 2) % 8 * 8 + col // 16) * 2 + col % 2
    rowp = (row == jnp.where(core == 0, col, swapped)).astype(BF16)
    chunk = row // 16
    line_of = (((chunk % NX + x_here) % NX) * NC + jnp.where(chunk < NX, core, 1 - core)) * 16 + row % 16
    colp = (col == line_of).astype(BF16)

    flows, contrib = core_call(
        labels, x_all, own, other, flow_pred, line_limit.reshape(1, -1), rowp, colp, nbus
    )

    half = lax.psum_scatter(
        contrib, AXES, scatter_dimension=0, tiled=True, axis_index_groups=MAJOR
    )
    last = lax.all_to_all(
        half.reshape(8, rows_here, nbus),
        AXES, split_axis=0, concat_axis=0, tiled=True, axis_index_groups=MINOR,
    )
    grad_injections = add_up(last)
    return (grad_injections, flows)


def solution(mesh):
    return jax.shard_map(
        per_device,
        mesh=mesh,
        in_specs=(
            P(("scen", "bus"), None),
            P("bus", "scen", None),
            P("bus"),
            P("bus"),
            P("scen", "bus"),
            P("bus"),
        ),
        out_specs=(P(("scen", "bus"), None), P("scen", "bus")),
        check_vma=False,
    )
```

```python
import jax
import jax.numpy as jnp
from jax import lax
from jax.experimental import pallas as pl
from jax.experimental.pallas import tpu as pltpu
from jax.sharding import PartitionSpec as P

AXES = ("scen", "bus")
NX = 4
NC = 2
NY = 8
NZ = 8
TILE = 128
LB = 3
BB = 2
CAP = 2
CODE_ROWS = 16
CHUNKS = 8
F32 = jnp.float32
BF16 = jnp.bfloat16


def dev(x, c, y, z):
    return ((x % NX) * NC + c) * (NY * NZ) + (y % NY) * NZ + (z % NZ)


def pairs(fn):
    return [
        (dev(x, c, y, z), fn(x, c, y, z))
        for x in range(NX)
        for c in range(NC)
        for y in range(NY)
        for z in range(NZ)
    ]


def ring_groups():
    minor, major = [], []
    for x in range(NX):
        for c in range(NC):
            for q in range(8):
                along_z = [dev(x, c, q, w) for w in range(NZ)]
                along_y = [dev(x, c, w, q) for w in range(NY)]
                minor.append(along_z if c == 0 else along_y)
                major.append(along_y if c == 0 else along_z)
    return minor, major


MINOR, MAJOR = ring_groups()
X_UP = pairs(lambda x, c, y, z: dev(x + 1, c, y, z))
X_DOWN = pairs(lambda x, c, y, z: dev(x - 1, c, y, z))
CORE_SWAP = pairs(lambda x, c, y, z: dev(x, 1 - c, y, z))


def pack_kernel(core_ref, line_ref, linev_ref, busv_ref, tiles_ref, x_ref, out_ref, count_ref):
    x_rows = x_ref.shape[0]
    head = x_rows + CODE_ROWS
    count = linev_ref.shape[1]
    row = lax.broadcasted_iota(jnp.int32, (CODE_ROWS, count), 0)
    code = jnp.where(row == 0, linev_ref[...], busv_ref[...]).astype(F32).astype(BF16)
    for m in range(out_ref.shape[0]):
        out_ref[m, :x_rows] = x_ref[...]
        out_ref[m, x_rows:head] = jnp.zeros((CODE_ROWS, TILE), BF16)
        out_ref[m, x_rows:head, :count] = code
        out_ref[m, head:] = jnp.zeros((out_ref.shape[1] - head, TILE), out_ref.dtype)
    for i in range(count_ref.shape[0]):
        count_ref[i] = 0
    rows = tiles_ref.shape[1]
    first_core = core_ref[0] == 0

    def body(t, carry):
        owner = lax.div(line_ref[t], LB)
        rank = count_ref[owner]
        count_ref[owner] = rank + 1
        y = owner >> 3
        z = owner & 7
        minor = jnp.where(first_core, z, y)
        major = jnp.where(first_core, y, z)
        at = pl.multiple_of(head + (major * CAP + rank) * rows, rows)
        out_ref[minor, pl.ds(at, rows)] = tiles_ref[t]
        return carry

    lax.fori_loop(0, tiles_ref.shape[0], body, 0, unroll=4)


def pack(core, tile_line, tile_bus, tile_values, x, owners):
    rows = tile_values.shape[1]
    total = x.shape[0] + CODE_ROWS + 8 * CAP * rows
    smem = pl.BlockSpec(memory_space=pltpu.SMEM)
    vmem = pl.BlockSpec(memory_space=pltpu.VMEM)
    return pl.pallas_call(
        pack_kernel,
        out_shape=jax.ShapeDtypeStruct((8, total, TILE), BF16),
        in_specs=[smem, smem, vmem, vmem, vmem, vmem],
        out_specs=vmem,
        scratch_shapes=[pltpu.SMEM((owners,), jnp.int32)],
        name="pack",
    )(core.reshape(1), tile_line, tile_line.reshape(1, -1), tile_bus.reshape(1, -1), tile_values, x)


def dot(a, b, dims):
    return lax.dot_general(a, b, (dims, ((), ())), preferred_element_type=F32)


NN = ((1,), (0,))
NT = ((1,), (1,))


def core_kernel(
    core_ref, label_ref, x_hbm, own_ref, other_ref, pred_ref, limit_ref, rowp_ref, colp_ref,
    flows_ref, c_hbm, x_ref, c_ref, acc_ref, g_ref, in_sem, out_sem,
):
    sources = label_ref.shape[0] // CAP
    step = sources // CHUNKS
    width = step * BB * TILE

    def bring(k):
        lanes = pl.ds(pl.multiple_of(k * width, width), width)
        return pltpu.make_async_copy(x_hbm.at[:, lanes], x_ref.at[:, lanes], in_sem.at[k])

    def leave(k):
        lanes = pl.ds(pl.multiple_of(k * width, width), width)
        return pltpu.make_async_copy(c_ref.at[:, lanes], c_hbm.at[:, lanes], out_sem.at[k])

    for k in range(CHUNKS):
        bring(k).start()

    first_core = core_ref[0] == 0

    def places(b):
        swapped = (b & 7) * 8 + (b >> 3)
        return jnp.where(first_core, b, swapped) * CAP, jnp.where(first_core, swapped, b) * CAP

    def tile(here, there):
        return jnp.concatenate(
            [own_ref[d, here] for d in range(NX)] + [other_ref[d, there] for d in range(NX)], axis=0
        )

    acc_ref[...] = jnp.zeros_like(acc_ref)

    def forward(k, carry):
        bring(k).wait()
        for i in range(step):
            here, there = places(k * step + i)
            for r in range(CAP):
                code = label_ref[here + r]
                line = code & 3
                start = pl.multiple_of((code >> 2) * TILE, TILE)
                part = dot(x_ref[:, pl.ds(start, TILE)], tile(here + r, there + r), NT)
                acc_ref[line] = acc_ref[line] + part
        return carry

    lax.fori_loop(0, CHUNKS, forward, 0)

    rowp = rowp_ref[...]
    colp = colp_ref[...]
    for b in range(LB):
        rest = acc_ref[b]
        flow = None
        for k in range(3):
            piece = rest.astype(BF16)
            rest = rest - piece.astype(F32)
            moved = dot(dot(rowp, piece, NN).astype(BF16), colp, NN)
            flow = moved if flow is None else flow + moved
        lanes = slice(b * TILE, (b + 1) * TILE)
        flows_ref[:, lanes] = flow
        cap = limit_ref[:, lanes].astype(F32) * 0.01
        grad = (
            (flow - pred_ref[:, lanes].astype(F32))
            + jax.nn.sigmoid(4.0 * (flow - cap))
            - jax.nn.sigmoid(4.0 * (-flow - cap))
        ).astype(BF16)
        grad = dot(rowp, grad, ((0,), (0,))).astype(BF16)
        g_ref[b] = dot(grad, colp, NT).astype(BF16)

    def backward(k, carry):
        for i in range(step):
            here, there = places(k * step + i)
            low = jnp.zeros((g_ref.shape[1], TILE), F32)
            high = low
            for r in range(CAP):
                code = label_ref[here + r]
                line = code & 3
                bus = (code >> 2) & 1
                part = dot(g_ref[line], tile(here + r, there + r), NN)
                low = low + jnp.where(bus == 0, part, 0.0)
                high = high + jnp.where(bus == 1, part, 0.0)
            start = pl.multiple_of((k * step + i) * (BB * TILE), BB * TILE)
            c_ref[:, pl.ds(start, BB * TILE)] = jnp.concatenate([low, high], axis=1).astype(BF16)
        leave(k).start()
        return carry

    lax.fori_loop(0, CHUNKS, backward, 0)
    for k in range(CHUNKS):
        leave(k).wait()


def core_call(core, labels, x, own, other, pred, limit, rowp, colp, nbus):
    rows, lines = pred.shape
    smem = pl.BlockSpec(memory_space=pltpu.SMEM)
    vmem = pl.BlockSpec(memory_space=pltpu.VMEM)
    anywhere = pl.BlockSpec(memory_space=pl.ANY)
    return pl.pallas_call(
        core_kernel,
        out_shape=(
            jax.ShapeDtypeStruct((rows, lines), F32),
            jax.ShapeDtypeStruct((rows, nbus), BF16),
        ),
        in_specs=[smem, smem, anywhere] + [vmem] * 6,
        out_specs=(vmem, anywhere),
        scratch_shapes=[
            pltpu.VMEM((rows, nbus), BF16),
            pltpu.VMEM((rows, nbus), BF16),
            pltpu.VMEM((LB, rows, TILE), F32),
            pltpu.VMEM((LB, rows, TILE), BF16),
            pltpu.SemaphoreType.DMA((CHUNKS,)),
            pltpu.SemaphoreType.DMA((CHUNKS,)),
        ],
        compiler_params=pltpu.CompilerParams(vmem_limit_bytes=32 * 1024 * 1024),
        name="flows_and_grad",
    )(core.reshape(1), labels, x, own, other, pred, limit, rowp, colp)


def add_up(parts):
    total = parts[0].astype(F32)
    for k in range(1, parts.shape[0]):
        total = total + parts[k].astype(F32)
    return total.astype(BF16)


def per_device(injections, tile_values, tile_line, tile_bus, flow_pred, line_limit):
    here = lax.axis_index("bus")
    scen = lax.axis_index("scen")
    x_here = scen // NC
    core = scen % NC
    buses = lax.axis_size("bus")
    rows_here, nbus = injections.shape
    count = tile_line.shape[0]

    blocks = nbus // TILE
    x_rows = rows_here * blocks
    flat = injections.reshape(rows_here, blocks, TILE).swapaxes(0, 1).reshape(x_rows, TILE)
    packed = pack(core, tile_line, tile_bus, tile_values, flat, buses)
    hop = lax.all_to_all(
        packed, AXES, split_axis=0, concat_axis=0, tiled=True, axis_index_groups=MINOR
    )
    near_x = hop[:, :x_rows].reshape(8, blocks, rows_here, TILE).swapaxes(1, 2)
    near_code = hop[:, x_rows : x_rows + rows_here].reshape(8 * rows_here, TILE)
    near = jnp.concatenate([near_x.reshape(8 * rows_here, nbus), near_code], axis=1)
    x_all = lax.all_gather(near, AXES, axis=0, tiled=True, axis_index_groups=MAJOR)

    slots = hop[:, x_rows + CODE_ROWS :].reshape((8, 8, CAP) + tile_values.shape[1:])
    mine = lax.all_to_all(
        slots.swapaxes(0, 1), AXES, split_axis=0, concat_axis=0, tiled=True, axis_index_groups=MAJOR
    ).reshape((buses * CAP,) + tile_values.shape[1:])
    from_below = lax.ppermute(mine, AXES, X_UP)
    from_above = lax.ppermute(mine, AXES, X_DOWN)
    from_far = lax.ppermute(from_below, AXES, X_UP)
    own = jnp.stack([mine, from_above, from_far, from_below])
    other = lax.ppermute(own, AXES, CORE_SWAP)

    tags = x_all[:, nbus:].astype(jnp.int32).reshape(buses, rows_here, TILE)
    line = tags[:, 0, :]
    inner = (line % LB) * BB + tags[:, 1, :]
    lane = lax.broadcasted_iota(jnp.int32, line.shape, 1)
    hit = (line // LB == here) & (lane < count)
    first = jnp.min(jnp.where(hit, lane, TILE), axis=1, keepdims=True)
    code_first = jnp.sum(jnp.where(lane == first, inner, 0), axis=1, keepdims=True)
    code_second = jnp.sum(jnp.where(hit, inner, 0), axis=1, keepdims=True) - code_first
    inner = jnp.concatenate([code_first, code_second], axis=1)
    order = lax.broadcasted_iota(jnp.int32, inner.shape, 0)
    source = jnp.where(core == 0, order, (order & 7) * 8 + (order >> 3))
    labels = (((source * BB + (inner & 1)) << 2) + (inner >> 1)).reshape(buses * CAP)

    row = lax.broadcasted_iota(jnp.int32, (TILE, TILE), 0)
    col = lax.broadcasted_iota(jnp.int32, (TILE, TILE), 1)
    swapped = ((col // 2) % 8 * 8 + col // 16) * 2 + col % 2
    rowp = (row == jnp.where(core == 0, col, swapped)).astype(BF16)
    chunk = row // 16
    line_of = (((chunk % NX + x_here) % NX) * NC + jnp.where(chunk < NX, core, 1 - core)) * 16 + row % 16
    colp = (col == line_of).astype(BF16)

    flows, contrib = core_call(
        core, labels, x_all, own, other, flow_pred, line_limit.reshape(1, -1), rowp, colp, nbus
    )

    half = lax.psum_scatter(
        contrib, AXES, scatter_dimension=0, tiled=True, axis_index_groups=MAJOR
    )
    last = lax.all_to_all(
        half.reshape(8, rows_here, nbus),
        AXES, split_axis=0, concat_axis=0, tiled=True, axis_index_groups=MINOR,
    )
    grad_injections = add_up(last)
    return (grad_injections, flows)


def solution(mesh):
    return jax.shard_map(
        per_device,
        mesh=mesh,
        in_specs=(
            P(("scen", "bus"), None),
            P("bus", "scen", None),
            P("bus"),
            P("bus"),
            P("scen", "bus"),
            P("bus"),
        ),
        out_specs=(P(("scen", "bus"), None), P("scen", "bus")),
        check_vma=False,
    )
```

```python
import jax
import jax.numpy as jnp
from jax import lax
from jax.experimental import pallas as pl
from jax.experimental.pallas import tpu as pltpu
from jax.sharding import PartitionSpec as P

AXES = ("scen", "bus")
NX = 4
NC = 2
NY = 8
NZ = 8
TILE = 128
LB = 3
BB = 2
CAP = 2
CODE_ROWS = 16
CHUNKS = 8
F32 = jnp.float32
BF16 = jnp.bfloat16


def dev(x, c, y, z):
    return ((x % NX) * NC + c) * (NY * NZ) + (y % NY) * NZ + (z % NZ)


def pairs(fn):
    return [
        (dev(x, c, y, z), fn(x, c, y, z))
        for x in range(NX)
        for c in range(NC)
        for y in range(NY)
        for z in range(NZ)
    ]


def ring_groups():
    minor, major = [], []
    for x in range(NX):
        for c in range(NC):
            for q in range(8):
                along_z = [dev(x, c, q, w) for w in range(NZ)]
                along_y = [dev(x, c, w, q) for w in range(NY)]
                minor.append(along_z if c == 0 else along_y)
                major.append(along_y if c == 0 else along_z)
    return minor, major


MINOR, MAJOR = ring_groups()
X_UP = pairs(lambda x, c, y, z: dev(x + 1, c, y, z))
X_DOWN = pairs(lambda x, c, y, z: dev(x - 1, c, y, z))
CORE_SWAP = pairs(lambda x, c, y, z: dev(x, 1 - c, y, z))


def pack_kernel(core_ref, line_ref, linev_ref, busv_ref, tiles_ref, x_ref, out_ref, count_ref):
    x_rows = x_ref.shape[0]
    head = x_rows + CODE_ROWS
    count = linev_ref.shape[1]
    row = lax.broadcasted_iota(jnp.int32, (CODE_ROWS, count), 0)
    code = jnp.where(row == 0, linev_ref[...], busv_ref[...]).astype(F32).astype(BF16)
    for m in range(out_ref.shape[0]):
        out_ref[m, :x_rows] = x_ref[...]
        out_ref[m, x_rows:head] = jnp.zeros((CODE_ROWS, TILE), BF16)
        out_ref[m, x_rows:head, :count] = code
        out_ref[m, head:] = jnp.zeros((out_ref.shape[1] - head, TILE), out_ref.dtype)
    for i in range(count_ref.shape[0]):
        count_ref[i] = 0
    rows = tiles_ref.shape[1]
    first_core = core_ref[0] == 0

    def body(t, carry):
        owner = lax.div(line_ref[t], LB)
        rank = count_ref[owner]
        count_ref[owner] = rank + 1
        y = owner >> 3
        z = owner & 7
        minor = jnp.where(first_core, z, y)
        major = jnp.where(first_core, y, z)
        at = pl.multiple_of(head + (major * CAP + rank) * rows, rows)
        out_ref[minor, pl.ds(at, rows)] = tiles_ref[t]
        return carry

    lax.fori_loop(0, tiles_ref.shape[0], body, 0, unroll=4)


def pack(core, tile_line, tile_bus, tile_values, x, owners):
    rows = tile_values.shape[1]
    total = x.shape[0] + CODE_ROWS + 8 * CAP * rows
    smem = pl.BlockSpec(memory_space=pltpu.SMEM)
    vmem = pl.BlockSpec(memory_space=pltpu.VMEM)
    return pl.pallas_call(
        pack_kernel,
        out_shape=jax.ShapeDtypeStruct((8, total, TILE), BF16),
        in_specs=[smem, smem, vmem, vmem, vmem, vmem],
        out_specs=vmem,
        scratch_shapes=[pltpu.SMEM((owners,), jnp.int32)],
        name="pack",
    )(core.reshape(1), tile_line, tile_line.reshape(1, -1), tile_bus.reshape(1, -1), tile_values, x)


def dot(a, b, dims):
    return lax.dot_general(a, b, (dims, ((), ())), preferred_element_type=F32)


NN = ((1,), (0,))
NT = ((1,), (1,))


def core_kernel(
    core_ref, label_ref, x_hbm, own_ref, own_far_ref, other_ref, other_far_ref, pred_ref, limit_ref, rowp_ref, colp_ref,
    flows_ref, c_hbm, x_ref, c_ref, acc_ref, g_ref, in_sem, out_sem,
):
    sources = label_ref.shape[0] // CAP
    step = sources // CHUNKS
    width = step * BB * TILE

    def bring(k):
        lanes = pl.ds(pl.multiple_of(k * width, width), width)
        return pltpu.make_async_copy(x_hbm.at[:, lanes], x_ref.at[:, lanes], in_sem.at[k])

    def leave(k):
        lanes = pl.ds(pl.multiple_of(k * width, width), width)
        return pltpu.make_async_copy(c_ref.at[:, lanes], c_hbm.at[:, lanes], out_sem.at[k])

    for k in range(CHUNKS):
        bring(k).start()

    first_core = core_ref[0] == 0

    def places(b):
        swapped = (b & 7) * 8 + (b >> 3)
        return jnp.where(first_core, b, swapped) * CAP, jnp.where(first_core, swapped, b) * CAP

    def tile(here, there):
        return jnp.concatenate(
            [own_ref[d, here] for d in range(NX - 1)]
            + [own_far_ref[here]]
            + [other_ref[d, there] for d in range(NX - 1)]
            + [other_far_ref[there]],
            axis=0,
        )

    acc_ref[...] = jnp.zeros_like(acc_ref)

    def forward(k, carry):
        bring(k).wait()
        for i in range(step):
            here, there = places(k * step + i)
            for r in range(CAP):
                code = label_ref[here + r]
                line = code & 3
                start = pl.multiple_of((code >> 2) * TILE, TILE)
                part = dot(x_ref[:, pl.ds(start, TILE)], tile(here + r, there + r), NT)
                acc_ref[line] = acc_ref[line] + part
        return carry

    lax.fori_loop(0, CHUNKS, forward, 0)

    rowp = rowp_ref[...]
    colp = colp_ref[...]
    for b in range(LB):
        rest = acc_ref[b]
        flow = None
        for k in range(3):
            piece = rest.astype(BF16)
            rest = rest - piece.astype(F32)
            moved = dot(dot(rowp, piece, NN).astype(BF16), colp, NN)
            flow = moved if flow is None else flow + moved
        lanes = slice(b * TILE, (b + 1) * TILE)
        flows_ref[:, lanes] = flow
        cap = limit_ref[:, lanes].astype(F32) * 0.01
        grad = (
            (flow - pred_ref[:, lanes].astype(F32))
            + jax.nn.sigmoid(4.0 * (flow - cap))
            - jax.nn.sigmoid(4.0 * (-flow - cap))
        ).astype(BF16)
        grad = dot(rowp, grad, ((0,), (0,))).astype(BF16)
        g_ref[b] = dot(grad, colp, NT).astype(BF16)

    def backward(k, carry):
        for i in range(step):
            here, there = places(k * step + i)
            low = jnp.zeros((g_ref.shape[1], TILE), F32)
            high = low
            for r in range(CAP):
                code = label_ref[here + r]
                line = code & 3
                bus = (code >> 2) & 1
                part = dot(g_ref[line], tile(here + r, there + r), NN)
                low = low + jnp.where(bus == 0, part, 0.0)
                high = high + jnp.where(bus == 1, part, 0.0)
            start = pl.multiple_of((k * step + i) * (BB * TILE), BB * TILE)
            c_ref[:, pl.ds(start, BB * TILE)] = jnp.concatenate([low, high], axis=1).astype(BF16)
        leave(k).start()
        return carry

    lax.fori_loop(0, CHUNKS, backward, 0)
    for k in range(CHUNKS):
        leave(k).wait()


def core_call(core, labels, x, own, own_far, other, other_far, pred, limit, rowp, colp, nbus):
    rows, lines = pred.shape
    smem = pl.BlockSpec(memory_space=pltpu.SMEM)
    vmem = pl.BlockSpec(memory_space=pltpu.VMEM)
    anywhere = pl.BlockSpec(memory_space=pltpu.HBM)
    return pl.pallas_call(
        core_kernel,
        out_shape=(
            jax.ShapeDtypeStruct((rows, lines), F32),
            jax.ShapeDtypeStruct((rows, nbus), BF16),
        ),
        in_specs=[smem, smem, anywhere] + [vmem] * 8,
        out_specs=(vmem, anywhere),
        scratch_shapes=[
            pltpu.VMEM((rows, nbus), BF16),
            pltpu.VMEM((rows, nbus), BF16),
            pltpu.VMEM((LB, rows, TILE), F32),
            pltpu.VMEM((LB, rows, TILE), BF16),
            pltpu.SemaphoreType.DMA((CHUNKS,)),
            pltpu.SemaphoreType.DMA((CHUNKS,)),
        ],
        compiler_params=pltpu.CompilerParams(vmem_limit_bytes=50 * 1024 * 1024),
        name="flows_and_grad",
    )(core.reshape(1), labels, x, own, own_far, other, other_far, pred, limit, rowp, colp)


def add_up(parts):
    total = parts[0].astype(F32)
    for k in range(1, parts.shape[0]):
        total = total + parts[k].astype(F32)
    return total.astype(BF16)


def per_device(injections, tile_values, tile_line, tile_bus, flow_pred, line_limit):
    here = lax.axis_index("bus")
    scen = lax.axis_index("scen")
    x_here = scen // NC
    core = scen % NC
    buses = lax.axis_size("bus")
    rows_here, nbus = injections.shape
    count = tile_line.shape[0]

    blocks = nbus // TILE
    x_rows = rows_here * blocks
    flat = injections.reshape(rows_here, blocks, TILE).swapaxes(0, 1).reshape(x_rows, TILE)
    packed = pack(core, tile_line, tile_bus, tile_values, flat, buses)
    hop = lax.all_to_all(
        packed, AXES, split_axis=0, concat_axis=0, tiled=True, axis_index_groups=MINOR
    )
    near_x = hop[:, :x_rows].reshape(8, blocks, rows_here, TILE).swapaxes(1, 2)
    near_code = hop[:, x_rows : x_rows + rows_here].reshape(8 * rows_here, TILE)
    near = jnp.concatenate([near_x.reshape(8 * rows_here, nbus), near_code], axis=1)
    x_all = lax.all_gather(near, AXES, axis=0, tiled=True, axis_index_groups=MAJOR)

    slots = hop[:, x_rows + CODE_ROWS :].reshape((8, 8, CAP) + tile_values.shape[1:])
    mine = lax.all_to_all(
        slots.swapaxes(0, 1), AXES, split_axis=0, concat_axis=0, tiled=True, axis_index_groups=MAJOR
    ).reshape((buses * CAP,) + tile_values.shape[1:])
    half_slots = mine.shape[0] // 2
    from_above = lax.ppermute(mine, AXES, X_DOWN)
    from_below = lax.ppermute(mine, AXES, X_UP)
    far = jnp.concatenate(
        [
            lax.ppermute(from_below[:half_slots], AXES, X_UP),
            lax.ppermute(from_above[half_slots:], AXES, X_DOWN),
        ],
        axis=0,
    )
    near3 = jnp.stack([mine, from_above, from_below])
    other3 = lax.ppermute(near3, AXES, CORE_SWAP)
    other_far = lax.ppermute(far, AXES, CORE_SWAP)

    tags = x_all[:, nbus:].astype(jnp.int32).reshape(buses, rows_here, TILE)
    line = tags[:, 0, :]
    inner = (line % LB) * BB + tags[:, 1, :]
    lane = lax.broadcasted_iota(jnp.int32, line.shape, 1)
    hit = (line // LB == here) & (lane < count)
    first = jnp.min(jnp.where(hit, lane, TILE), axis=1, keepdims=True)
    code_first = jnp.sum(jnp.where(lane == first, inner, 0), axis=1, keepdims=True)
    code_second = jnp.sum(jnp.where(hit, inner, 0), axis=1, keepdims=True) - code_first
    inner = jnp.concatenate([code_first, code_second], axis=1)
    order = lax.broadcasted_iota(jnp.int32, inner.shape, 0)
    source = jnp.where(core == 0, order, (order & 7) * 8 + (order >> 3))
    labels = (((source * BB + (inner & 1)) << 2) + (inner >> 1)).reshape(buses * CAP)

    row = lax.broadcasted_iota(jnp.int32, (TILE, TILE), 0)
    col = lax.broadcasted_iota(jnp.int32, (TILE, TILE), 1)
    swapped = ((col // 2) % 8 * 8 + col // 16) * 2 + col % 2
    rowp = (row == jnp.where(core == 0, col, swapped)).astype(BF16)
    chunk = row // 16
    piece = chunk % NX
    offset = jnp.where(piece < 2, piece, 5 - piece)
    line_of = (((offset + x_here) % NX) * NC + jnp.where(chunk < NX, core, 1 - core)) * 16 + row % 16
    colp = (col == line_of).astype(BF16)

    flows, contrib = core_call(
        core, labels, x_all, near3, far, other3, other_far, flow_pred, line_limit.reshape(1, -1), rowp, colp, nbus
    )

    half = lax.psum_scatter(
        contrib, AXES, scatter_dimension=0, tiled=True, axis_index_groups=MAJOR
    )
    last = lax.all_to_all(
        half.reshape(8, rows_here, nbus),
        AXES, split_axis=0, concat_axis=0, tiled=True, axis_index_groups=MINOR,
    )
    grad_injections = add_up(last)
    return (grad_injections, flows)


def solution(mesh):
    return jax.shard_map(
        per_device,
        mesh=mesh,
        in_specs=(
            P(("scen", "bus"), None),
            P("bus", "scen", None),
            P("bus"),
            P("bus"),
            P("scen", "bus"),
            P("bus"),
        ),
        out_specs=(P(("scen", "bus"), None), P("scen", "bus")),
        check_vma=False,
    )
```

```python
import jax
import jax.numpy as jnp
from jax import lax
from jax.experimental import pallas as pl
from jax.experimental.pallas import tpu as pltpu
from jax.sharding import PartitionSpec as P

AXES = ("scen", "bus")
NX = 4
NC = 2
NY = 8
NZ = 8
TILE = 128
LB = 3
BB = 2
CAP = 2
CODE_ROWS = 16
CHUNKS = 8
AHEAD = 2
F32 = jnp.float32
BF16 = jnp.bfloat16


def dev(x, c, y, z):
    return ((x % NX) * NC + c) * (NY * NZ) + (y % NY) * NZ + (z % NZ)


def pairs(fn):
    return [
        (dev(x, c, y, z), fn(x, c, y, z))
        for x in range(NX)
        for c in range(NC)
        for y in range(NY)
        for z in range(NZ)
    ]


def ring_groups():
    minor, major = [], []
    for x in range(NX):
        for c in range(NC):
            for q in range(8):
                along_z = [dev(x, c, q, w) for w in range(NZ)]
                along_y = [dev(x, c, w, q) for w in range(NY)]
                minor.append(along_z if c == 0 else along_y)
                major.append(along_y if c == 0 else along_z)
    return minor, major


MINOR, MAJOR = ring_groups()
X_UP = pairs(lambda x, c, y, z: dev(x + 1, c, y, z))
X_DOWN = pairs(lambda x, c, y, z: dev(x - 1, c, y, z))
CORE_SWAP = pairs(lambda x, c, y, z: dev(x, 1 - c, y, z))


def pack_kernel(core_ref, line_ref, linev_ref, busv_ref, tiles_ref, x_ref, out_ref, count_ref):
    x_rows = x_ref.shape[0]
    head = x_rows + CODE_ROWS
    count = linev_ref.shape[1]
    row = lax.broadcasted_iota(jnp.int32, (CODE_ROWS, count), 0)
    code = jnp.where(row == 0, linev_ref[...], busv_ref[...]).astype(F32).astype(BF16)
    for m in range(out_ref.shape[0]):
        out_ref[m, :x_rows] = x_ref[...]
        out_ref[m, x_rows:head] = jnp.zeros((CODE_ROWS, TILE), BF16)
        out_ref[m, x_rows:head, :count] = code
        out_ref[m, head:] = jnp.zeros((out_ref.shape[1] - head, TILE), out_ref.dtype)
    for i in range(count_ref.shape[0]):
        count_ref[i] = 0
    rows = tiles_ref.shape[1]
    first_core = core_ref[0] == 0

    def body(t, carry):
        owner = lax.div(line_ref[t], LB)
        rank = count_ref[owner]
        count_ref[owner] = rank + 1
        y = owner >> 3
        z = owner & 7
        minor = jnp.where(first_core, z, y)
        major = jnp.where(first_core, y, z)
        at = pl.multiple_of(head + (major * CAP + rank) * rows, rows)
        out_ref[minor, pl.ds(at, rows)] = tiles_ref[t]
        return carry

    lax.fori_loop(0, tiles_ref.shape[0], body, 0, unroll=4)


def pack(core, tile_line, tile_bus, tile_values, x, owners):
    rows = tile_values.shape[1]
    total = x.shape[0] + CODE_ROWS + 8 * CAP * rows
    smem = pl.BlockSpec(memory_space=pltpu.SMEM)
    vmem = pl.BlockSpec(memory_space=pltpu.VMEM)
    return pl.pallas_call(
        pack_kernel,
        out_shape=jax.ShapeDtypeStruct((8, total, TILE), BF16),
        in_specs=[smem, smem, vmem, vmem, vmem, vmem],
        out_specs=vmem,
        scratch_shapes=[pltpu.SMEM((owners,), jnp.int32)],
        name="pack",
    )(core.reshape(1), tile_line, tile_line.reshape(1, -1), tile_bus.reshape(1, -1), tile_values, x)


def dot(a, b, dims):
    return lax.dot_general(a, b, (dims, ((), ())), preferred_element_type=F32)


NN = ((1,), (0,))
NT = ((1,), (1,))


def core_kernel(
    core_ref, label_ref, x_hbm, own_ref, own_far_ref, other_ref, other_far_ref, pred_ref, limit_ref, rowp_ref, colp_ref,
    flows_ref, c_hbm, x_ref, c_ref, acc_ref, g_ref, in_sem, out_sem,
):
    sources = label_ref.shape[0] // CAP
    step = sources // CHUNKS
    width = step * BB * TILE

    def bring(k):
        lanes = pl.ds(pl.multiple_of(k * width, width), width)
        return pltpu.make_async_copy(x_hbm.at[:, lanes], x_ref.at[:, lanes], in_sem.at[k])

    def leave(k):
        lanes = pl.ds(pl.multiple_of(k * width, width), width)
        return pltpu.make_async_copy(c_ref.at[:, lanes], c_hbm.at[:, lanes], out_sem.at[k])

    for k in range(AHEAD):
        bring(k).start()

    first_core = core_ref[0] == 0

    def places(b):
        swapped = (b & 7) * 8 + (b >> 3)
        return jnp.where(first_core, b, swapped) * CAP, jnp.where(first_core, swapped, b) * CAP

    def tile(here, there):
        return jnp.concatenate(
            [own_ref[d, here] for d in range(NX - 1)]
            + [own_far_ref[here]]
            + [other_ref[d, there] for d in range(NX - 1)]
            + [other_far_ref[there]],
            axis=0,
        )

    acc_ref[...] = jnp.zeros_like(acc_ref)

    def forward(k, carry):
        bring(k).wait()

        @pl.when(k + AHEAD < CHUNKS)
        def _():
            bring(k + AHEAD).start()

        for i in range(step):
            here, there = places(k * step + i)
            for r in range(CAP):
                code = label_ref[here + r]
                line = code & 3
                start = pl.multiple_of((code >> 2) * TILE, TILE)
                part = dot(x_ref[:, pl.ds(start, TILE)], tile(here + r, there + r), NT)
                acc_ref[line] = acc_ref[line] + part
        return carry

    lax.fori_loop(0, CHUNKS, forward, 0)

    rowp = rowp_ref[...]
    colp = colp_ref[...]
    for b in range(LB):
        rest = acc_ref[b]
        flow = None
        for k in range(3):
            piece = rest.astype(BF16)
            rest = rest - piece.astype(F32)
            moved = dot(dot(rowp, piece, NN).astype(BF16), colp, NN)
            flow = moved if flow is None else flow + moved
        lanes = slice(b * TILE, (b + 1) * TILE)
        flows_ref[:, lanes] = flow
        cap = limit_ref[:, lanes].astype(F32) * 0.01
        grad = (
            (flow - pred_ref[:, lanes].astype(F32))
            + jax.nn.sigmoid(4.0 * (flow - cap))
            - jax.nn.sigmoid(4.0 * (-flow - cap))
        ).astype(BF16)
        grad = dot(rowp, grad, ((0,), (0,))).astype(BF16)
        g_ref[b] = dot(grad, colp, NT).astype(BF16)

    def backward(k, carry):
        for i in range(step):
            here, there = places(k * step + i)
            low = jnp.zeros((g_ref.shape[1], TILE), F32)
            high = low
            for r in range(CAP):
                code = label_ref[here + r]
                line = code & 3
                bus = (code >> 2) & 1
                part = dot(g_ref[line], tile(here + r, there + r), NN)
                low = low + jnp.where(bus == 0, part, 0.0)
                high = high + jnp.where(bus == 1, part, 0.0)
            start = pl.multiple_of((k * step + i) * (BB * TILE), BB * TILE)
            c_ref[:, pl.ds(start, BB * TILE)] = jnp.concatenate([low, high], axis=1).astype(BF16)
        leave(k).start()
        return carry

    lax.fori_loop(0, CHUNKS, backward, 0)
    for k in range(CHUNKS):
        leave(k).wait()


def core_call(core, labels, x, own, own_far, other, other_far, pred, limit, rowp, colp, nbus):
    rows, lines = pred.shape
    smem = pl.BlockSpec(memory_space=pltpu.SMEM)
    vmem = pl.BlockSpec(memory_space=pltpu.VMEM)
    anywhere = pl.BlockSpec(memory_space=pltpu.HBM)
    return pl.pallas_call(
        core_kernel,
        out_shape=(
            jax.ShapeDtypeStruct((rows, lines), F32),
            jax.ShapeDtypeStruct((rows, nbus), BF16),
        ),
        in_specs=[smem, smem, anywhere] + [vmem] * 8,
        out_specs=(vmem, anywhere),
        scratch_shapes=[
            pltpu.VMEM((rows, nbus), BF16),
            pltpu.VMEM((rows, nbus), BF16),
            pltpu.VMEM((LB, rows, TILE), F32),
            pltpu.VMEM((LB, rows, TILE), BF16),
            pltpu.SemaphoreType.DMA((CHUNKS,)),
            pltpu.SemaphoreType.DMA((CHUNKS,)),
        ],
        compiler_params=pltpu.CompilerParams(vmem_limit_bytes=50 * 1024 * 1024),
        name="flows_and_grad",
    )(core.reshape(1), labels, x, own, own_far, other, other_far, pred, limit, rowp, colp)


def add_up(parts):
    total = parts[0].astype(F32)
    for k in range(1, parts.shape[0]):
        total = total + parts[k].astype(F32)
    return total.astype(BF16)


def per_device(injections, tile_values, tile_line, tile_bus, flow_pred, line_limit):
    here = lax.axis_index("bus")
    scen = lax.axis_index("scen")
    x_here = scen // NC
    core = scen % NC
    buses = lax.axis_size("bus")
    rows_here, nbus = injections.shape
    count = tile_line.shape[0]

    blocks = nbus // TILE
    x_rows = rows_here * blocks
    flat = injections.reshape(rows_here, blocks, TILE).swapaxes(0, 1).reshape(x_rows, TILE)
    packed = pack(core, tile_line, tile_bus, tile_values, flat, buses)
    hop = lax.all_to_all(
        packed, AXES, split_axis=0, concat_axis=0, tiled=True, axis_index_groups=MINOR
    )
    near_x = hop[:, :x_rows].reshape(8, blocks, rows_here, TILE).swapaxes(1, 2)
    near_code = hop[:, x_rows : x_rows + rows_here].reshape(8 * rows_here, TILE)
    near = jnp.concatenate([near_x.reshape(8 * rows_here, nbus), near_code], axis=1)
    x_all = lax.all_gather(near, AXES, axis=0, tiled=True, axis_index_groups=MAJOR)

    slots = hop[:, x_rows + CODE_ROWS :].reshape((8, 8, CAP) + tile_values.shape[1:])
    mine = lax.all_to_all(
        slots.swapaxes(0, 1), AXES, split_axis=0, concat_axis=0, tiled=True, axis_index_groups=MAJOR
    ).reshape((buses * CAP,) + tile_values.shape[1:])
    from_below = lax.ppermute(mine, AXES, X_UP)
    from_above = lax.ppermute(mine, AXES, X_DOWN)
    far = lax.ppermute(from_below, AXES, X_UP)
    near3 = jnp.stack([mine, from_above, from_below])
    other3 = lax.ppermute(near3, AXES, CORE_SWAP)
    other_far = lax.ppermute(far, AXES, CORE_SWAP)

    tags = x_all[:, nbus:].astype(jnp.int32).reshape(buses, rows_here, TILE)
    line = tags[:, 0, :]
    inner = (line % LB) * BB + tags[:, 1, :]
    lane = lax.broadcasted_iota(jnp.int32, line.shape, 1)
    hit = (line // LB == here) & (lane < count)
    first = jnp.min(jnp.where(hit, lane, TILE), axis=1, keepdims=True)
    code_first = jnp.sum(jnp.where(lane == first, inner, 0), axis=1, keepdims=True)
    code_second = jnp.sum(jnp.where(hit, inner, 0), axis=1, keepdims=True) - code_first
    inner = jnp.concatenate([code_first, code_second], axis=1)
    order = lax.broadcasted_iota(jnp.int32, inner.shape, 0)
    source = jnp.where(core == 0, order, (order & 7) * 8 + (order >> 3))
    labels = (((source * BB + (inner & 1)) << 2) + (inner >> 1)).reshape(buses * CAP)

    row = lax.broadcasted_iota(jnp.int32, (TILE, TILE), 0)
    col = lax.broadcasted_iota(jnp.int32, (TILE, TILE), 1)
    swapped = ((col // 2) % 8 * 8 + col // 16) * 2 + col % 2
    rowp = (row == jnp.where(core == 0, col, swapped)).astype(BF16)
    chunk = row // 16
    piece = chunk % NX
    offset = jnp.where(piece < 2, piece, 5 - piece)
    line_of = (((offset + x_here) % NX) * NC + jnp.where(chunk < NX, core, 1 - core)) * 16 + row % 16
    colp = (col == line_of).astype(BF16)

    flows, contrib = core_call(
        core, labels, x_all, near3, far, other3, other_far, flow_pred, line_limit.reshape(1, -1), rowp, colp, nbus
    )

    half = lax.psum_scatter(
        contrib, AXES, scatter_dimension=0, tiled=True, axis_index_groups=MAJOR
    )
    last = lax.all_to_all(
        half.reshape(8, rows_here, nbus),
        AXES, split_axis=0, concat_axis=0, tiled=True, axis_index_groups=MINOR,
    )
    grad_injections = add_up(last)
    return (grad_injections, flows)


def solution(mesh):
    return jax.shard_map(
        per_device,
        mesh=mesh,
        in_specs=(
            P(("scen", "bus"), None),
            P("bus", "scen", None),
            P("bus"),
            P("bus"),
            P("scen", "bus"),
            P("bus"),
        ),
        out_specs=(P(("scen", "bus"), None), P("scen", "bus")),
        check_vma=False,
    )
```

```python
import jax
import jax.numpy as jnp
from jax import lax
from jax.experimental import pallas as pl
from jax.experimental.pallas import tpu as pltpu
from jax.sharding import PartitionSpec as P

AXES = ("scen", "bus")
NX = 4
NC = 2
NY = 8
NZ = 8
TILE = 128
LB = 3
BB = 2
CAP = 2
CODE_ROWS = 16
CHUNKS = 8
F32 = jnp.float32
BF16 = jnp.bfloat16


def dev(x, c, y, z):
    return ((x % NX) * NC + c) * (NY * NZ) + (y % NY) * NZ + (z % NZ)


def pairs(fn):
    return [
        (dev(x, c, y, z), fn(x, c, y, z))
        for x in range(NX)
        for c in range(NC)
        for y in range(NY)
        for z in range(NZ)
    ]


def ring_groups():
    minor, major = [], []
    for x in range(NX):
        for c in range(NC):
            for q in range(8):
                along_z = [dev(x, c, q, w) for w in range(NZ)]
                along_y = [dev(x, c, w, q) for w in range(NY)]
                minor.append(along_z if c == 0 else along_y)
                major.append(along_y if c == 0 else along_z)
    return minor, major


MINOR, MAJOR = ring_groups()
X_UP = pairs(lambda x, c, y, z: dev(x + 1, c, y, z))
X_DOWN = pairs(lambda x, c, y, z: dev(x - 1, c, y, z))
CORE_SWAP = pairs(lambda x, c, y, z: dev(x, 1 - c, y, z))


def pack_kernel(core_ref, line_ref, linev_ref, busv_ref, tiles_ref, x_ref, out_ref, count_ref):
    x_rows = x_ref.shape[0]
    head = x_rows + CODE_ROWS
    count = linev_ref.shape[1]
    row = lax.broadcasted_iota(jnp.int32, (CODE_ROWS, count), 0)
    code = jnp.where(row == 0, linev_ref[...], busv_ref[...]).astype(F32).astype(BF16)
    for m in range(out_ref.shape[0]):
        out_ref[m, :x_rows] = x_ref[...]
        out_ref[m, x_rows:head] = jnp.zeros((CODE_ROWS, TILE), BF16)
        out_ref[m, x_rows:head, :count] = code
        out_ref[m, head:] = jnp.zeros((out_ref.shape[1] - head, TILE), out_ref.dtype)
    for i in range(count_ref.shape[0]):
        count_ref[i] = 0
    rows = tiles_ref.shape[1]
    first_core = core_ref[0] == 0

    def body(t, carry):
        owner = lax.div(line_ref[t], LB)
        rank = count_ref[owner]
        count_ref[owner] = rank + 1
        y = owner >> 3
        z = owner & 7
        minor = jnp.where(first_core, z, y)
        major = jnp.where(first_core, y, z)
        at = pl.multiple_of(head + (major * CAP + rank) * rows, rows)
        out_ref[minor, pl.ds(at, rows)] = tiles_ref[t]
        return carry

    lax.fori_loop(0, tiles_ref.shape[0], body, 0, unroll=4)


def pack(core, tile_line, tile_bus, tile_values, x, owners):
    rows = tile_values.shape[1]
    total = x.shape[0] + CODE_ROWS + 8 * CAP * rows
    smem = pl.BlockSpec(memory_space=pltpu.SMEM)
    vmem = pl.BlockSpec(memory_space=pltpu.VMEM)
    return pl.pallas_call(
        pack_kernel,
        out_shape=jax.ShapeDtypeStruct((8, total, TILE), BF16),
        in_specs=[smem, smem, vmem, vmem, vmem, vmem],
        out_specs=vmem,
        scratch_shapes=[pltpu.SMEM((owners,), jnp.int32)],
        name="pack",
    )(core.reshape(1), tile_line, tile_line.reshape(1, -1), tile_bus.reshape(1, -1), tile_values, x)


def dot(a, b, dims):
    return lax.dot_general(a, b, (dims, ((), ())), preferred_element_type=F32)


NN = ((1,), (0,))
NT = ((1,), (1,))


def core_kernel(
    core_ref, label_ref, x_hbm, own0, own1, own2, own3, other0, other1, other2, other3,
    pred_ref, limit_ref, rowp_ref, colp_ref, flows_ref, c_hbm, x_ref, c_ref, acc_ref, g_ref, in_sem, out_sem,
):
    sources = label_ref.shape[0] // CAP
    step = sources // CHUNKS
    width = step * BB * TILE

    def bring(k):
        lanes = pl.ds(pl.multiple_of(k * width, width), width)
        return pltpu.make_async_copy(x_hbm.at[:, lanes], x_ref.at[:, lanes], in_sem.at[k])

    def leave(k):
        lanes = pl.ds(pl.multiple_of(k * width, width), width)
        return pltpu.make_async_copy(c_ref.at[:, lanes], c_hbm.at[:, lanes], out_sem.at[k])

    for k in range(CHUNKS):
        bring(k).start()

    first_core = core_ref[0] == 0

    def places(b):
        swapped = (b & 7) * 8 + (b >> 3)
        return jnp.where(first_core, b, swapped) * CAP, jnp.where(first_core, swapped, b) * CAP

    def tile(here, there):
        return jnp.concatenate(
            [ref[here] for ref in (own0, own1, own2, own3)]
            + [ref[there] for ref in (other0, other1, other2, other3)],
            axis=0,
        )

    acc_ref[...] = jnp.zeros_like(acc_ref)

    def forward(k, carry):
        bring(k).wait()
        for i in range(step):
            here, there = places(k * step + i)
            for r in range(CAP):
                code = label_ref[here + r]
                line = code & 3
                start = pl.multiple_of((code >> 2) * TILE, TILE)
                part = dot(x_ref[:, pl.ds(start, TILE)], tile(here + r, there + r), NT)
                acc_ref[line] = acc_ref[line] + part
        return carry

    lax.fori_loop(0, CHUNKS, forward, 0)

    rowp = rowp_ref[...]
    colp = colp_ref[...]
    for b in range(LB):
        rest = acc_ref[b]
        flow = None
        for k in range(3):
            piece = rest.astype(BF16)
            rest = rest - piece.astype(F32)
            moved = dot(dot(rowp, piece, NN).astype(BF16), colp, NN)
            flow = moved if flow is None else flow + moved
        lanes = slice(b * TILE, (b + 1) * TILE)
        flows_ref[:, lanes] = flow
        cap = limit_ref[:, lanes].astype(F32) * 0.01
        grad = (
            (flow - pred_ref[:, lanes].astype(F32))
            + jax.nn.sigmoid(4.0 * (flow - cap))
            - jax.nn.sigmoid(4.0 * (-flow - cap))
        ).astype(BF16)
        grad = dot(rowp, grad, ((0,), (0,))).astype(BF16)
        g_ref[b] = dot(grad, colp, NT).astype(BF16)

    def backward(k, carry):
        for i in range(step):
            here, there = places(k * step + i)
            low = jnp.zeros((g_ref.shape[1], TILE), F32)
            high = low
            for r in range(CAP):
                code = label_ref[here + r]
                line = code & 3
                bus = (code >> 2) & 1
                part = dot(g_ref[line], tile(here + r, there + r), NN)
                low = low + jnp.where(bus == 0, part, 0.0)
                high = high + jnp.where(bus == 1, part, 0.0)
            start = pl.multiple_of((k * step + i) * (BB * TILE), BB * TILE)
            c_ref[:, pl.ds(start, BB * TILE)] = jnp.concatenate([low, high], axis=1).astype(BF16)
        leave(k).start()
        return carry

    lax.fori_loop(0, CHUNKS, backward, 0)
    for k in range(CHUNKS):
        leave(k).wait()


def core_call(core, labels, x, pieces, pred, limit, rowp, colp, nbus):
    rows, lines = pred.shape
    smem = pl.BlockSpec(memory_space=pltpu.SMEM)
    vmem = pl.BlockSpec(memory_space=pltpu.VMEM)
    anywhere = pl.BlockSpec(memory_space=pltpu.HBM)
    return pl.pallas_call(
        core_kernel,
        out_shape=(
            jax.ShapeDtypeStruct((rows, lines), F32),
            jax.ShapeDtypeStruct((rows, nbus), BF16),
        ),
        in_specs=[smem, smem, anywhere] + [vmem] * (2 * NX + 4),
        out_specs=(vmem, anywhere),
        scratch_shapes=[
            pltpu.VMEM((rows, nbus), BF16),
            pltpu.VMEM((rows, nbus), BF16),
            pltpu.VMEM((LB, rows, TILE), F32),
            pltpu.VMEM((LB, rows, TILE), BF16),
            pltpu.SemaphoreType.DMA((CHUNKS,)),
            pltpu.SemaphoreType.DMA((CHUNKS,)),
        ],
        compiler_params=pltpu.CompilerParams(vmem_limit_bytes=46 * 1024 * 1024),
        name="flows_and_grad",
    )(core.reshape(1), labels, x, *pieces, pred, limit, rowp, colp)


def add_up(parts):
    total = parts[0].astype(F32)
    for k in range(1, parts.shape[0]):
        total = total + parts[k].astype(F32)
    return total.astype(BF16)


def per_device(injections, tile_values, tile_line, tile_bus, flow_pred, line_limit):
    here = lax.axis_index("bus")
    scen = lax.axis_index("scen")
    x_here = scen // NC
    core = scen % NC
    buses = lax.axis_size("bus")
    rows_here, nbus = injections.shape
    count = tile_line.shape[0]

    blocks = nbus // TILE
    x_rows = rows_here * blocks
    flat = injections.reshape(rows_here, blocks, TILE).swapaxes(0, 1).reshape(x_rows, TILE)
    packed = pack(core, tile_line, tile_bus, tile_values, flat, buses)
    hop = lax.all_to_all(
        packed, AXES, split_axis=0, concat_axis=0, tiled=True, axis_index_groups=MINOR
    )
    near_x = hop[:, :x_rows].reshape(8, blocks, rows_here, TILE).swapaxes(1, 2)
    near_code = hop[:, x_rows : x_rows + rows_here].reshape(8 * rows_here, TILE)
    near = jnp.concatenate([near_x.reshape(8 * rows_here, nbus), near_code], axis=1)
    x_all = lax.all_gather(near, AXES, axis=0, tiled=True, axis_index_groups=MAJOR)

    slots = hop[:, x_rows + CODE_ROWS :].reshape((8, 8, CAP) + tile_values.shape[1:])
    mine = lax.all_to_all(
        slots.swapaxes(0, 1), AXES, split_axis=0, concat_axis=0, tiled=True, axis_index_groups=MAJOR
    ).reshape((buses * CAP,) + tile_values.shape[1:])
    from_below = lax.ppermute(mine, AXES, X_UP)
    from_above = lax.ppermute(mine, AXES, X_DOWN)
    far = lax.ppermute(from_below, AXES, X_UP)
    pieces = (mine, from_above, from_below, far)
    pieces = pieces + tuple(lax.ppermute(p, AXES, CORE_SWAP) for p in pieces)

    tags = x_all[:, nbus:].astype(jnp.int32).reshape(buses, rows_here, TILE)
    line = tags[:, 0, :]
    inner = (line % LB) * BB + tags[:, 1, :]
    lane = lax.broadcasted_iota(jnp.int32, line.shape, 1)
    hit = (line // LB == here) & (lane < count)
    first = jnp.min(jnp.where(hit, lane, TILE), axis=1, keepdims=True)
    code_first = jnp.sum(jnp.where(lane == first, inner, 0), axis=1, keepdims=True)
    code_second = jnp.sum(jnp.where(hit, inner, 0), axis=1, keepdims=True) - code_first
    inner = jnp.concatenate([code_first, code_second], axis=1)
    order = lax.broadcasted_iota(jnp.int32, inner.shape, 0)
    source = jnp.where(core == 0, order, (order & 7) * 8 + (order >> 3))
    labels = (((source * BB + (inner & 1)) << 2) + (inner >> 1)).reshape(buses * CAP)

    row = lax.broadcasted_iota(jnp.int32, (TILE, TILE), 0)
    col = lax.broadcasted_iota(jnp.int32, (TILE, TILE), 1)
    swapped = ((col // 2) % 8 * 8 + col // 16) * 2 + col % 2
    rowp = (row == jnp.where(core == 0, col, swapped)).astype(BF16)
    chunk = row // 16
    piece = chunk % NX
    offset = jnp.where(piece < 2, piece, 5 - piece)
    line_of = (((offset + x_here) % NX) * NC + jnp.where(chunk < NX, core, 1 - core)) * 16 + row % 16
    colp = (col == line_of).astype(BF16)

    flows, contrib = core_call(
        core, labels, x_all, pieces, flow_pred, line_limit.reshape(1, -1), rowp, colp, nbus
    )

    half = lax.psum_scatter(
        contrib, AXES, scatter_dimension=0, tiled=True, axis_index_groups=MAJOR
    )
    last = lax.all_to_all(
        half.reshape(8, rows_here, nbus),
        AXES, split_axis=0, concat_axis=0, tiled=True, axis_index_groups=MINOR,
    )
    grad_injections = add_up(last)
    return (grad_injections, flows)


def solution(mesh):
    return jax.shard_map(
        per_device,
        mesh=mesh,
        in_specs=(
            P(("scen", "bus"), None),
            P("bus", "scen", None),
            P("bus"),
            P("bus"),
            P("scen", "bus"),
            P("bus"),
        ),
        out_specs=(P(("scen", "bus"), None), P("scen", "bus")),
        check_vma=False,
    )
```

```python
import jax
import jax.numpy as jnp
from jax import lax
from jax.experimental import pallas as pl
from jax.experimental.pallas import tpu as pltpu
from jax.sharding import PartitionSpec as P

AXES = ("scen", "bus")
NX = 4
NC = 2
NY = 8
NZ = 8
TILE = 128
LB = 3
BB = 2
CAP = 2
CODE_ROWS = 16
CHUNKS = 8
F32 = jnp.float32
BF16 = jnp.bfloat16


def dev(x, c, y, z):
    return ((x % NX) * NC + c) * (NY * NZ) + (y % NY) * NZ + (z % NZ)


def pairs(fn):
    return [
        (dev(x, c, y, z), fn(x, c, y, z))
        for x in range(NX)
        for c in range(NC)
        for y in range(NY)
        for z in range(NZ)
    ]


def ring_groups():
    minor, major = [], []
    for x in range(NX):
        for c in range(NC):
            for q in range(8):
                along_z = [dev(x, c, q, w) for w in range(NZ)]
                along_y = [dev(x, c, w, q) for w in range(NY)]
                minor.append(along_z if c == 0 else along_y)
                major.append(along_y if c == 0 else along_z)
    return minor, major


MINOR, MAJOR = ring_groups()
X_UP = pairs(lambda x, c, y, z: dev(x + 1, c, y, z))
X_DOWN = pairs(lambda x, c, y, z: dev(x - 1, c, y, z))
CORE_SWAP = pairs(lambda x, c, y, z: dev(x, 1 - c, y, z))


def pack_kernel(core_ref, line_ref, linev_ref, busv_ref, tiles_ref, x_ref, out_ref, count_ref):
    x_rows = x_ref.shape[0]
    head = x_rows + CODE_ROWS
    count = linev_ref.shape[1]
    row = lax.broadcasted_iota(jnp.int32, (CODE_ROWS, count), 0)
    code = jnp.where(row == 0, linev_ref[...], busv_ref[...]).astype(F32).astype(BF16)
    for m in range(out_ref.shape[0]):
        out_ref[m, :x_rows] = x_ref[...]
        out_ref[m, x_rows:head] = jnp.zeros((CODE_ROWS, TILE), BF16)
        out_ref[m, x_rows:head, :count] = code
        out_ref[m, head:] = jnp.zeros((out_ref.shape[1] - head, TILE), out_ref.dtype)
    for i in range(count_ref.shape[0]):
        count_ref[i] = 0
    rows = tiles_ref.shape[1]
    first_core = core_ref[0] == 0

    def body(t, carry):
        owner = lax.div(line_ref[t], LB)
        rank = count_ref[owner]
        count_ref[owner] = rank + 1
        y = owner >> 3
        z = owner & 7
        minor = jnp.where(first_core, z, y)
        major = jnp.where(first_core, y, z)
        at = pl.multiple_of(head + (major * CAP + rank) * rows, rows)
        out_ref[minor, pl.ds(at, rows)] = tiles_ref[t]
        return carry

    lax.fori_loop(0, tiles_ref.shape[0], body, 0, unroll=4)


def pack(core, tile_line, tile_bus, tile_values, x, owners):
    rows = tile_values.shape[1]
    total = x.shape[0] + CODE_ROWS + 8 * CAP * rows
    smem = pl.BlockSpec(memory_space=pltpu.SMEM)
    vmem = pl.BlockSpec(memory_space=pltpu.VMEM)
    return pl.pallas_call(
        pack_kernel,
        out_shape=jax.ShapeDtypeStruct((8, total, TILE), BF16),
        in_specs=[smem, smem, vmem, vmem, vmem, vmem],
        out_specs=vmem,
        scratch_shapes=[pltpu.SMEM((owners,), jnp.int32)],
        name="pack",
    )(core.reshape(1), tile_line, tile_line.reshape(1, -1), tile_bus.reshape(1, -1), tile_values, x)


def dot(a, b, dims):
    return lax.dot_general(a, b, (dims, ((), ())), preferred_element_type=F32)


NN = ((1,), (0,))
NT = ((1,), (1,))


def core_kernel(
    core_ref, label_ref, x_hbm, own0, own1, own2, own3, other0, other1, other2, other3,
    pred_ref, limit_ref, rowp_ref, colp_ref, flows_ref, c_hbm, x_ref, c_ref, acc_ref, g_ref, in_sem, out_sem,
):
    sources = label_ref.shape[0] // CAP
    step = sources // CHUNKS
    width = step * BB * TILE

    def bring(k):
        lanes = pl.ds(pl.multiple_of(k * width, width), width)
        return pltpu.make_async_copy(x_hbm.at[:, lanes], x_ref.at[:, lanes], in_sem.at[k])

    def leave(k):
        lanes = pl.ds(pl.multiple_of(k * width, width), width)
        return pltpu.make_async_copy(c_ref.at[:, lanes], c_hbm.at[:, lanes], out_sem.at[k])

    for k in range(CHUNKS):
        bring(k).start()

    first_core = core_ref[0] == 0

    def places(b):
        swapped = (b & 7) * 8 + (b >> 3)
        return jnp.where(first_core, b, swapped) * CAP, jnp.where(first_core, swapped, b) * CAP

    def tile(here, there):
        return jnp.concatenate(
            [ref[here] for ref in (own0, own1, own2, own3)]
            + [ref[there] for ref in (other0, other1, other2, other3)],
            axis=0,
        )

    acc_ref[...] = jnp.zeros_like(acc_ref)

    def forward(k, carry):
        bring(k).wait()
        for i in range(step):
            here, there = places(k * step + i)
            for r in range(CAP):
                code = label_ref[here + r]
                line = code & 3
                start = pl.multiple_of((code >> 2) * TILE, TILE)
                part = dot(x_ref[:, pl.ds(start, TILE)], tile(here + r, there + r), NT)
                acc_ref[line] = acc_ref[line] + part
        return carry

    lax.fori_loop(0, CHUNKS, forward, 0, unroll=2)

    rowp = rowp_ref[...]
    colp = colp_ref[...]
    for b in range(LB):
        rest = acc_ref[b]
        flow = None
        for k in range(3):
            piece = rest.astype(BF16)
            rest = rest - piece.astype(F32)
            moved = dot(dot(rowp, piece, NN).astype(BF16), colp, NN)
            flow = moved if flow is None else flow + moved
        lanes = slice(b * TILE, (b + 1) * TILE)
        flows_ref[:, lanes] = flow
        cap = limit_ref[:, lanes].astype(F32) * 0.01
        grad = (
            (flow - pred_ref[:, lanes].astype(F32))
            + jax.nn.sigmoid(4.0 * (flow - cap))
            - jax.nn.sigmoid(4.0 * (-flow - cap))
        ).astype(BF16)
        grad = dot(rowp, grad, ((0,), (0,))).astype(BF16)
        g_ref[b] = dot(grad, colp, NT).astype(BF16)

    def backward(k, carry):
        for i in range(step):
            here, there = places(k * step + i)
            low = jnp.zeros((g_ref.shape[1], TILE), F32)
            high = low
            for r in range(CAP):
                code = label_ref[here + r]
                line = code & 3
                bus = (code >> 2) & 1
                part = dot(g_ref[line], tile(here + r, there + r), NN)
                low = low + jnp.where(bus == 0, part, 0.0)
                high = high + jnp.where(bus == 1, part, 0.0)
            start = pl.multiple_of((k * step + i) * (BB * TILE), BB * TILE)
            c_ref[:, pl.ds(start, BB * TILE)] = jnp.concatenate([low, high], axis=1).astype(BF16)
        leave(k).start()
        return carry

    lax.fori_loop(0, CHUNKS, backward, 0, unroll=2)
    for k in range(CHUNKS):
        leave(k).wait()


def core_call(core, labels, x, pieces, pred, limit, rowp, colp, nbus):
    rows, lines = pred.shape
    smem = pl.BlockSpec(memory_space=pltpu.SMEM)
    vmem = pl.BlockSpec(memory_space=pltpu.VMEM)
    anywhere = pl.BlockSpec(memory_space=pltpu.HBM)
    return pl.pallas_call(
        core_kernel,
        out_shape=(
            jax.ShapeDtypeStruct((rows, lines), F32),
            jax.ShapeDtypeStruct((rows, nbus), BF16),
        ),
        in_specs=[smem, smem, anywhere] + [vmem] * (2 * NX + 4),
        out_specs=(vmem, anywhere),
        scratch_shapes=[
            pltpu.VMEM((rows, nbus), BF16),
            pltpu.VMEM((rows, nbus), BF16),
            pltpu.VMEM((LB, rows, TILE), F32),
            pltpu.VMEM((LB, rows, TILE), BF16),
            pltpu.SemaphoreType.DMA((CHUNKS,)),
            pltpu.SemaphoreType.DMA((CHUNKS,)),
        ],
        compiler_params=pltpu.CompilerParams(vmem_limit_bytes=46 * 1024 * 1024),
        name="flows_and_grad",
    )(core.reshape(1), labels, x, *pieces, pred, limit, rowp, colp)


def add_up(parts):
    total = parts[0].astype(F32)
    for k in range(1, parts.shape[0]):
        total = total + parts[k].astype(F32)
    return total.astype(BF16)


def per_device(injections, tile_values, tile_line, tile_bus, flow_pred, line_limit):
    here = lax.axis_index("bus")
    scen = lax.axis_index("scen")
    x_here = scen // NC
    core = scen % NC
    buses = lax.axis_size("bus")
    rows_here, nbus = injections.shape
    count = tile_line.shape[0]

    blocks = nbus // TILE
    x_rows = rows_here * blocks
    flat = injections.reshape(rows_here, blocks, TILE).swapaxes(0, 1).reshape(x_rows, TILE)
    packed = pack(core, tile_line, tile_bus, tile_values, flat, buses)
    hop = lax.all_to_all(
        packed, AXES, split_axis=0, concat_axis=0, tiled=True, axis_index_groups=MINOR
    )
    near_x = hop[:, :x_rows].reshape(8, blocks, rows_here, TILE).swapaxes(1, 2)
    near_code = hop[:, x_rows : x_rows + rows_here].reshape(8 * rows_here, TILE)
    near = jnp.concatenate([near_x.reshape(8 * rows_here, nbus), near_code], axis=1)
    x_all = lax.all_gather(near, AXES, axis=0, tiled=True, axis_index_groups=MAJOR)

    slots = hop[:, x_rows + CODE_ROWS :].reshape((8, 8, CAP) + tile_values.shape[1:])
    mine = lax.all_to_all(
        slots.swapaxes(0, 1), AXES, split_axis=0, concat_axis=0, tiled=True, axis_index_groups=MAJOR
    ).reshape((buses * CAP,) + tile_values.shape[1:])
    from_below = lax.ppermute(mine, AXES, X_UP)
    from_above = lax.ppermute(mine, AXES, X_DOWN)
    far = lax.ppermute(from_below, AXES, X_UP)
    pieces = (mine, from_above, from_below, far)
    pieces = pieces + tuple(lax.ppermute(p, AXES, CORE_SWAP) for p in pieces)

    tags = x_all[:, nbus:].astype(jnp.int32).reshape(buses, rows_here, TILE)
    line = tags[:, 0, :]
    inner = (line % LB) * BB + tags[:, 1, :]
    lane = lax.broadcasted_iota(jnp.int32, line.shape, 1)
    hit = (line // LB == here) & (lane < count)
    first = jnp.min(jnp.where(hit, lane, TILE), axis=1, keepdims=True)
    code_first = jnp.sum(jnp.where(lane == first, inner, 0), axis=1, keepdims=True)
    code_second = jnp.sum(jnp.where(hit, inner, 0), axis=1, keepdims=True) - code_first
    inner = jnp.concatenate([code_first, code_second], axis=1)
    order = lax.broadcasted_iota(jnp.int32, inner.shape, 0)
    source = jnp.where(core == 0, order, (order & 7) * 8 + (order >> 3))
    labels = (((source * BB + (inner & 1)) << 2) + (inner >> 1)).reshape(buses * CAP)

    row = lax.broadcasted_iota(jnp.int32, (TILE, TILE), 0)
    col = lax.broadcasted_iota(jnp.int32, (TILE, TILE), 1)
    swapped = ((col // 2) % 8 * 8 + col // 16) * 2 + col % 2
    rowp = (row == jnp.where(core == 0, col, swapped)).astype(BF16)
    chunk = row // 16
    piece = chunk % NX
    offset = jnp.where(piece < 2, piece, 5 - piece)
    line_of = (((offset + x_here) % NX) * NC + jnp.where(chunk < NX, core, 1 - core)) * 16 + row % 16
    colp = (col == line_of).astype(BF16)

    flows, contrib = core_call(
        core, labels, x_all, pieces, flow_pred, line_limit.reshape(1, -1), rowp, colp, nbus
    )

    half = lax.psum_scatter(
        contrib, AXES, scatter_dimension=0, tiled=True, axis_index_groups=MAJOR
    )
    last = lax.all_to_all(
        half.reshape(8, rows_here, nbus),
        AXES, split_axis=0, concat_axis=0, tiled=True, axis_index_groups=MINOR,
    )
    grad_injections = add_up(last)
    return (grad_injections, flows)


def solution(mesh):
    return jax.shard_map(
        per_device,
        mesh=mesh,
        in_specs=(
            P(("scen", "bus"), None),
            P("bus", "scen", None),
            P("bus"),
            P("bus"),
            P("scen", "bus"),
            P("bus"),
        ),
        out_specs=(P(("scen", "bus"), None), P("scen", "bus")),
        check_vma=False,
    )
```
